128 devices in a mesh: group: 4 (over x), dev: 32 (over y, z, core).
Axes of the slice: x: 4, y: 4, z: 4, core: 2. Of those that a mesh axis runs over, the one named last changes fastest.
Arguments:
- source: float32 [64, 1024, 256], P('group', 'dev'), may hold values from -6 to 6
- plane_layer: int32 [256], replicated, may hold values from 0 to 7
- layer_permittivity: float32 [8], replicated, may hold values from 1 to 12
- tile_kind: int32 [8, 128], replicated, may hold values from 0 to 15
- kind_fill: float32 [16], replicated, may hold values from 0.5 to 2
Outputs:
- potential: float32 [64, 1024, 256], P('group', 'dev')
- residual: float32 [64, 1024, 256], P('group', 'dev')
The draws below stay inside these ranges and needn't reach their ends.
All inputs are finite; a program needn't handle non-finite values.
Results may differ from the reference program's by a relative error of at most 0.00015.
Values sent between devices are 32-bit elements; how exact they have to be, the bound alone decides.
A program may use at most 192 MiB of HBM per device.

```python
import math
import jax
import jax.numpy as jnp
from jax import lax

NZ = 256
DEPTH = 5
COARSE_SWEEPS = 24
TILE = 8
LAYERS = 8
KINDS = 16
NX = 64
NY = 1024
TX = 8
TY = 128


def draw_source(key, part):
    return jnp.clip(jax.random.normal(key, (NX, NY, NZ), jnp.float32), -6.0, 6.0)


def touch_ends(entries, stream_key, smallest, largest):
    dims = entries.shape
    place = [jax.random.randint(jax.random.fold_in(stream_key, axis), (), 0, dims[axis]) for axis in range(len(dims))]
    entries = entries.at[tuple(place)].set(smallest)
    longest = dims.index(max(dims))
    place[longest] = (place[longest] + 1) % dims[longest]
    return entries.at[tuple(place)].set(largest)


def setup_inputs(seed: int = 0) -> dict:
    arg_keys = jax.random.split(jax.random.key(seed), 6)
    source = draw_source(jax.random.fold_in(arg_keys[5], 71), 0)
    plane_layer = touch_ends(jax.random.randint(arg_keys[1], (NZ,), 0, LAYERS), jax.random.fold_in(arg_keys[1], 1), 0, LAYERS - 1).astype(jnp.int32)
    layer_permittivity = jnp.clip(jnp.exp(jax.random.uniform(arg_keys[2], (LAYERS,), jnp.float32, math.log(1.0), math.log(12.0))), 1.0, 12.0)
    tile_kind = touch_ends(jax.random.randint(arg_keys[3], (TX, TY), 0, KINDS), jax.random.fold_in(arg_keys[3], 1), 0, KINDS - 1).astype(jnp.int32)
    kind_fill = jnp.clip(jnp.exp(jax.random.uniform(arg_keys[4], (KINDS,), jnp.float32, math.log(0.5), math.log(2.0))), 0.5, 2.0)
    return dict(source=source, plane_layer=plane_layer, layer_permittivity=layer_permittivity, tile_kind=tile_kind, kind_fill=kind_fill)


omega_damp = 2.0 / 3.0
NEIGHBOUR_SLICES = (
    (slice(2, None), slice(1, -1), slice(1, -1)),
    (slice(0, -2), slice(1, -1), slice(1, -1)),
    (slice(1, -1), slice(2, None), slice(1, -1)),
    (slice(1, -1), slice(0, -2), slice(1, -1)),
    (slice(1, -1), slice(1, -1), slice(2, None)),
    (slice(1, -1), slice(1, -1), slice(0, -2)),
)


def padded_z(array_in):
    return jnp.pad(array_in, ((0, 0), (0, 0), (1, 1)))


def pad_xy(array_in, circle_width):
    return jnp.pad(array_in, ((circle_width, circle_width), (circle_width, circle_width), (0, 0)))


def stencil(value_ext, coeff_ext):
    val_pad = padded_z(value_ext)
    coef_pad = padded_z(coeff_ext)
    centre = val_pad[1:-1, 1:-1, 1:-1]
    coeff_mid = coef_pad[1:-1, 1:-1, 1:-1]
    accum = jnp.zeros_like(centre)
    for where_at in NEIGHBOUR_SLICES:
        accum = accum + (coeff_mid + coef_pad[where_at]) * (centre - val_pad[where_at])
    return 0.5 * accum


def diagonal(coeff_ext):
    coef_pad = padded_z(coeff_ext)
    accum = 6.0 * coef_pad[1:-1, 1:-1, 1:-1]
    for where_at in NEIGHBOUR_SLICES:
        accum = accum + coef_pad[where_at]
    return 0.5 * accum


def relax(value_ext, coeff_ext, source_now, diag_vals, level_scale):
    centre = value_ext[1:-1, 1:-1]
    return centre + omega_damp * (source_now - level_scale * stencil(value_ext, coeff_ext)) / diag_vals


def restrict(array_in):
    size_x, size_y, size_z = array_in.shape
    return array_in.reshape(size_x // 2, 2, size_y // 2, 2, size_z // 2, 2).sum(axis=(1, 3, 5)) * 0.125


def prolong(array_in):
    size_x, size_y, size_z = array_in.shape
    spread = jnp.broadcast_to(array_in[:, None, :, None, :, None], (size_x, 2, size_y, 2, size_z, 2))
    return spread.reshape(2 * size_x, 2 * size_y, 2 * size_z)


def coarse_fill(fill_level):
    size_x, size_y = fill_level.shape
    return fill_level.reshape(size_x // 2, 2, size_y // 2, 2).sum(axis=(1, 3)) * 0.25


def coarse_permit(permit_level):
    return permit_level.reshape(-1, 2).sum(axis=1) * 0.5


def global_cycle(depth_now, source_now, fill_level, permit_level):
    level_scale = 0.25 ** depth_now
    coeff_ext = pad_xy(fill_level[:, :, None] * permit_level[None, None, :], 1)
    diag_vals = level_scale * diagonal(coeff_ext)
    iterate = omega_damp * source_now / diag_vals
    if depth_now == DEPTH:
        def sweep_once(step_num, current):
            return relax(pad_xy(current, 1), coeff_ext, source_now, diag_vals, level_scale)
        return lax.fori_loop(0, COARSE_SWEEPS - 1, sweep_once, iterate)
    iterate = relax(pad_xy(iterate, 1), coeff_ext, source_now, diag_vals, level_scale)
    leftover = source_now - level_scale * stencil(pad_xy(iterate, 1), coeff_ext)
    correction = global_cycle(depth_now + 1, restrict(leftover), coarse_fill(fill_level), coarse_permit(permit_level))
    iterate = iterate + prolong(correction)
    iterate = relax(pad_xy(iterate, 1), coeff_ext, source_now, diag_vals, level_scale)
    iterate = relax(pad_xy(iterate, 1), coeff_ext, source_now, diag_vals, level_scale)
    return iterate


def reference(source, plane_layer, layer_permittivity, tile_kind, kind_fill):
    permit = layer_permittivity[plane_layer]
    fill_map = jnp.repeat(jnp.repeat(kind_fill[tile_kind], TILE, axis=0), TILE, axis=1)
    potential = global_cycle(0, source, fill_map, permit)
    coeff_top = pad_xy(fill_map[:, :, None] * permit[None, None, :], 1)
    residual = source - 1.0 * stencil(pad_xy(potential, 1), coeff_top)
    return potential, residual
```

```python
import functools

import jax
import jax.numpy as jnp
from jax import lax
from jax.experimental import pallas as pl
from jax.experimental.pallas import tpu as pltpu
from jax.sharding import PartitionSpec as P

MESH = pl.DeviceIdType.MESH
OMEGA = 2.0 / 3.0
KEEP = 1.0 - OMEGA
SWEEPS = 24
NEIGHBOURS = tuple(
    (dx, dy) for dx in (-1, 0, 1) for dy in (-1, 0, 1) if (dx, dy) != (0, 0)
)


def kernel(
    groups,
    devs,
    layers_ref,
    kinds_ref,
    permit_ref,
    fill_ref,
    source,
    pot_ref,
    res_ref,
    F0, V0, W0, B0, INV0, A0, AXP0, AXM0, AYP0, AYM0, RF0, HF0, FX0, T0, P0,
    F1, V1, W1, B1, INV1, A1, AXP1, AXM1, AYP1, AYM1, RF1, HF1, FX1, T1, P1,
    F2, V2, W2, B2, INV2, A2, AXP2, AXM2, AYP2, AYM2, RF2, HF2, FX2, UU,
    FA, G, F4, F5, FC, VC, WC, BC, INVC, AC, AXPC, AXMC, AYPC, AYMC,
    local_sem, s0_send, s0_recv, s0l_send, s0l_recv, s1_send, s1_recv, s1l_send, s1l_recv,
    s2_send, s2_recv, s3_send, s3_recv,
):
    g = lax.axis_index("group")
    d = lax.axis_index("dev")
    f32 = jnp.float32
    lane = lax.broadcasted_iota(jnp.int32, (8, 128), 1)
    sub = lax.broadcasted_iota(jnp.int32, (8, 128), 0)
    even = (lane & 1) == 0

    def peer(dx, dy):
        return (lax.rem(g + dx + groups, groups), lax.rem(d + dy + devs, devs))

    def roll(v, shift):
        return pltpu.roll(v, shift % 128, 1)

    def sroll(v, shift):
        return pltpu.roll(v, shift % 8, 0)

    barrier = pltpu.get_barrier_semaphore()
    group_offsets = tuple(range(1, groups))
    column = [(dx, dy) for dx in range(groups) for dy in (-1, 0, 1) if (dx, dy) != (0, 0)]
    for dx, dy in column:
        pl.semaphore_signal(barrier, inc=1, device_id=peer(dx, dy), device_id_type=MESH)

    def greet(k, carry):
        pl.semaphore_signal(barrier, inc=1, device_id=(g, lax.rem(d + k, devs)), device_id_type=MESH)
        return carry

    lax.fori_loop(2, devs - 1, greet, 0)
    own = [
        pltpu.make_async_copy(
            source.at[:, :, h * 128 : h * 128 + 128], F0.at[h, 4:20, 8:40, :], local_sem.at[h]
        )
        for h in range(2)
    ]
    for copy in own:
        copy.start()
    pl.semaphore_wait(barrier, len(column) + devs - 3)

    def halo0(dx, dy, h, late):
        px = {0: (0, 16, 4), 1: (14, 2, 2), -1: (0, 2, 20)}[dx]
        if late:
            px = {1: (12, 2, 0), -1: (2, 2, 22)}[dx]
        py = {0: (0, 32, 8), 1: (24, 8, 0), -1: (0, 8, 40)}[dy]
        slot = ((dx + 1) * 3 + dy + 1) * 2 + h
        send, recv = (s0l_send, s0l_recv) if late else (s0_send, s0_recv)
        return pltpu.make_async_remote_copy(
            src_ref=source.at[px[0] : px[0] + px[1], py[0] : py[0] + py[1], h * 128 : h * 128 + 128],
            dst_ref=F0.at[h, px[2] : px[2] + px[1], py[2] : py[2] + py[1], :],
            send_sem=send.at[slot],
            recv_sem=recv.at[slot],
            device_id=peer(dx, dy),
            device_id_type=MESH,
        )

    first0 = [halo0(dx, dy, h, False) for dx, dy in NEIGHBOURS for h in range(2)]
    late0 = [halo0(dx, dy, h, True) for dx, dy in NEIGHBOURS if dx for h in range(2)]
    for copy in first0:
        copy.start()

    def halo1(dx, dy, late):
        px = {0: (0, 8, 5), 1: (6, 2, 3), -1: (0, 2, 13)}[dx]
        if late:
            px = {1: (3, 3, 0), -1: (2, 3, 15)}[dx]
        py = {0: (0, 16, 8), 1: (8, 8, 0), -1: (0, 8, 24)}[dy]
        slot = (dx + 1) * 3 + dy + 1
        send, recv = (s1l_send, s1l_recv) if late else (s1_send, s1_recv)
        return pltpu.make_async_remote_copy(
            src_ref=F1.at[px[0] + 5 : px[0] + px[1] + 5, py[0] + 8 : py[0] + py[1] + 8, :],
            dst_ref=F1.at[px[2] : px[2] + px[1], py[2] : py[2] + py[1], :],
            send_sem=send.at[slot],
            recv_sem=recv.at[slot],
            device_id=peer(dx, dy),
            device_id_type=MESH,
        )

    first1 = [halo1(dx, dy, False) for dx, dy in NEIGHBOURS]
    late1 = [halo1(dx, dy, True) for dx, dy in NEIGHBOURS if dx]

    def block2(slot):
        dx, dy = column[slot]
        return pltpu.make_async_remote_copy(
            src_ref=F2.at[pl.ds(4 * g, 4), 8:16, :],
            dst_ref=F2.at[pl.ds(4 * g, 4), 8 - 8 * dy : 16 - 8 * dy, :],
            send_sem=s2_send.at[slot],
            recv_sem=s2_recv.at[slot],
            device_id=peer(dx, dy),
            device_id_type=MESH,
        )

    first2 = [block2(slot) for slot in range(len(column))]

    kinds = kinds_ref[...]
    fills = jnp.zeros((8, 128), f32)
    for kind in range(fill_ref.shape[0]):
        fills = jnp.where(kinds == kind, fill_ref[kind], fills)
    fills = jnp.where(lane < 4 * devs, fills, 0.0)
    shifted = pltpu.roll(fills, lax.rem(8 + 128 - 4 * d + 128, 128), 1)
    tile_y = 4 * d - 8 + lane
    shifted = jnp.where((tile_y >= 0) & (tile_y < 4 * devs), shifted, 0.0)
    zero = jnp.zeros((8, 128), f32)
    for c in range(3):
        for x in (0, 1, 10, 11):
            FA[x, 8 * c : 8 * c + 8, :] = zero
        for x in range(8):
            row = jnp.broadcast_to(shifted[x : x + 1, :], (8, 128))
            picked = jnp.sum(jnp.where(lane == sub + 8 * c, row, 0.0), axis=1, keepdims=True)
            FA[x + 2, 8 * c : 8 * c + 8, :] = jnp.broadcast_to(picked, (8, 128))

    permit0 = []
    for h in range(2):
        layer = jnp.broadcast_to(layers_ref[h : h + 1, :], (8, 128))
        value = jnp.zeros((8, 128), f32)
        for k in range(permit_ref.shape[0]):
            value = jnp.where(layer == k, permit_ref[k], value)
        permit0.append(value)

    def zup0(h0, h1):
        r0, r1 = roll(h0, -1), roll(h1, -1)
        return jnp.where(lane == 127, r1, r0), r1

    def zdn0(h0, h1):
        r0, r1 = roll(h0, 1), roll(h1, 1)
        return r0, jnp.where(lane == 0, r0, r1)

    def zup(v, level):
        step = 1 << level
        return jnp.where(lane >= 128 - step, roll(v, -(step + 1)), roll(v, -step))

    def zdn(v, level):
        step = 1 << level
        return jnp.where(lane < step, roll(v, step + 1), roll(v, step))

    def pair(v, step):
        return v + jnp.where((lane & step) == 0, roll(v, -step), roll(v, step))

    def spair(v, step):
        return v + jnp.where((sub & step) == 0, sroll(v, -step), sroll(v, step))

    def halves(h0, h1):
        return jnp.where(even, h0, h1) + jnp.where(even, roll(h0, -1), roll(h1, 1))

    pu0, pu1 = zup0(*permit0)
    pd0, pd1 = zdn0(*permit0)
    RP0 = [1.0 / p for p in permit0]
    ru = [pu0 * RP0[0], jnp.where(lane == 127, 0.0, pu1 * RP0[1])]
    rd = [jnp.where(lane == 0, 0.0, pd0 * RP0[0]), pd1 * RP0[1]]
    BU0 = [1.0 + ru[0], jnp.where(lane == 127, 0.0, 1.0 + ru[1])]
    BD0 = [jnp.where(lane == 0, 0.0, 1.0 + rd[0]), 1.0 + rd[1]]
    BS0 = [2.0 + ru[h] + rd[h] for h in range(2)]
    permits = [None, 0.5 * halves(*permit0)]
    for level in (2, 3, 4, 5):
        permits.append(0.5 * pair(permits[level - 1], 1 << (level - 1)))
    RPS, BU, BD, BS = [None], [None], [None], [None]
    for level in range(1, 6):
        p = permits[level]
        step = 1 << level
        rp = 1.0 / p
        top = (lane >= 128 - step) & ((lane & 1) == 1)
        bottom = (lane < step) & even
        up = jnp.where(top, 0.0, zup(p, level) * rp)
        dn = jnp.where(bottom, 0.0, zdn(p, level) * rp)
        RPS.append(rp)
        BU.append(jnp.where(top, 0.0, 1.0 + up))
        BD.append(jnp.where(bottom, 0.0, 1.0 + dn))
        BS.append(2.0 + up + dn)

    for t in range(6):
        for j in range(8):
            FX0[t, 8 * j : 8 * j + 8, :] = jnp.broadcast_to(FA[2 * g + t, 6 + j : 7 + j, :], (8, 128))

    def weights0(c, carry):
        at = pl.multiple_of(8 * c, 8)
        out = pl.ds(at, 8)
        for t in range(4):
            f = FX0[t + 1, pl.ds(at + 12, 8), :]
            inside = f > 0.0
            rf = 1.0 / jnp.where(inside, f, 1.0)
            ryp = FX0[t + 1, pl.ds(at + 13, 8), :] * rf
            rym = FX0[t + 1, pl.ds(at + 11, 8), :] * rf
            rxp = FX0[t + 2, pl.ds(at + 12, 8), :] * rf
            rxm = FX0[t, pl.ds(at + 12, 8), :] * rf
            AYP0[t, out, :] = 1.0 + ryp
            AYM0[t, out, :] = 1.0 + rym
            RF0[t, out, :] = 2.0 * rf
            HF0[t, out, :] = 0.5 * f
            ry = 4.0 + ryp + rym
            for kind in range(3):
                if (t, kind) in ((0, 0), (3, 2)):
                    continue
                rp = rxp if kind == 2 else jnp.ones_like(rxp)
                rm = rxm if kind == 0 else jnp.ones_like(rxm)
                AXP0[3 * t + kind, out, :] = 1.0 + rp
                AXM0[3 * t + kind, out, :] = 1.0 + rm
                a = ry + rp + rm
                A0[3 * t + kind, out, :] = a
                for h in range(2):
                    INV0[h, 3 * t + kind, out, :] = jnp.where(inside, OMEGA / (a + BS0[h]), 0.0)
        return carry

    lax.fori_loop(0, 5, weights0, 0)

    for t in range(6):
        for j in range(6):
            FX1[t, 8 * j : 8 * j + 8, :] = jnp.where(
                sub < 4,
                jnp.broadcast_to(FA[2 * g + t, 4 + 2 * j : 5 + 2 * j, :], (8, 128)),
                jnp.broadcast_to(FA[2 * g + t, 5 + 2 * j : 6 + 2 * j, :], (8, 128)),
            )

    def weights1(c, carry):
        at = pl.multiple_of(8 * c, 8)
        out = pl.ds(at, 8)
        for t in range(6):
            f = FX1[t, pl.ds(at + 8, 8), :]
            inside = f > 0.0
            rf = 1.0 / jnp.where(inside, f, 1.0)
            ryp = FX1[t, pl.ds(at + 9, 8), :] * rf
            rym = FX1[t, pl.ds(at + 7, 8), :] * rf
            AYP1[t, out, :] = 1.0 + ryp
            AYM1[t, out, :] = 1.0 + rym
            RF1[t, out, :] = 8.0 * rf
            HF1[t, out, :] = 0.125 * f
            ry = 4.0 + ryp + rym
            for r in range(4):
                q = 4 * t + r - 3
                if q < 0 or q > 17:
                    continue
                rp = FX1[t + 1, pl.ds(at + 8, 8), :] * rf if r == 3 else jnp.ones_like(rf)
                rm = FX1[t - 1, pl.ds(at + 8, 8), :] * rf if r == 0 else jnp.ones_like(rf)
                AXP1[q, out, :] = 1.0 + rp
                AXM1[q, out, :] = 1.0 + rm
                a = ry + rp + rm
                A1[q, out, :] = a
                INV1[q, out, :] = jnp.where(inside, OMEGA / (a + BS[1]), 0.0)
        return carry

    lax.fori_loop(0, 4, weights1, 0)

    for copy in own:
        copy.wait()
    for copy in first0:
        copy.wait_recv()

    def kind0(q):
        t = (q + 4) // 8
        r = (q + 4) % 8
        return t, 3 * t + (r + 6) // 7 + r // 7

    def start0(q, carry):
        t, kind = kind0(q)
        for c in range(5):
            rows = pl.ds(8 * c, 8)
            rf = RF0[t, rows, :]
            for h in range(2):
                f = F0[h, q, pl.ds(8 * c + 4, 8), :]
                B0[h, q, pl.ds(8 * c + 8, 8), :] = f * INV0[h, kind, rows, :] * (rf * RP0[h])
        return carry

    def spread0(v_ref, q, t, kind, row, w_row):
        axp, axm = AXP0[kind, pl.ds(w_row, 8), :], AXM0[kind, pl.ds(w_row, 8), :]
        ayp, aym = AYP0[t, pl.ds(w_row, 8), :], AYM0[t, pl.ds(w_row, 8), :]
        centre = [v_ref[h, q, pl.ds(row, 8), :] for h in range(2)]
        up, dn = zup0(*centre), zdn0(*centre)
        total = []
        for h in range(2):
            total.append(
                axp * v_ref[h, q + 1, pl.ds(row, 8), :]
                + axm * v_ref[h, q - 1, pl.ds(row, 8), :]
                + ayp * v_ref[h, q, pl.ds(row + 1, 8), :]
                + aym * v_ref[h, q, pl.ds(row - 1, 8), :]
                + BU0[h] * up[h]
                + BD0[h] * dn[h]
            )
        return centre, total

    def relax0(src, dst, fresh):
        def body(q, carry):
            t, kind = kind0(q)
            for c in range(5):
                row = 8 * c + 8
                centre, total = spread0(src, q, t, kind, row, 8 * c)
                for h in range(2):
                    if fresh:
                        kept = (1.0 + KEEP) * centre[h]
                    else:
                        kept = KEEP * centre[h] + B0[h, q, pl.ds(row, 8), :]
                    dst[h, q, pl.ds(row, 8), :] = kept + INV0[h, kind, pl.ds(8 * c, 8), :] * total[h]
            return carry

        return body

    def left0(v_ref, q, c):
        t, kind = kind0(q)
        w_row = 8 * c + 4
        centre, total = spread0(v_ref, q, t, kind, 8 * c + 12, w_row)
        a = A0[kind, pl.ds(w_row, 8), :]
        hf = HF0[t, pl.ds(w_row, 8), :]
        left = []
        for h in range(2):
            f = F0[h, q, pl.ds(8 * c + 8, 8), :]
            left.append(f - hf * permit0[h] * ((a + BS0[h]) * centre[h] - total[h]))
        return centre, left

    lax.fori_loop(2, 22, start0, 0)
    lax.fori_loop(3, 21, relax0(B0, V0, True), 0)

    def down0(i, carry):
        for c in range(4):
            first = left0(V0, 2 * i + 4, c)[1]
            second = left0(V0, 2 * i + 5, c)[1]
            T0[i, pl.ds(8 * c, 8), :] = halves(first[0] + second[0], first[1] + second[1])
        F1[i + 5, 8:24, :] = 0.125 * (
            T0[i, pl.ds(0, 16, stride=2), :] + T0[i, pl.ds(1, 16, stride=2), :]
        )
        return carry

    lax.fori_loop(0, 8, down0, 0)
    for copy in first1 + late0:
        copy.start()

    for x in range(10):
        for j in range(5):
            rows = [jnp.broadcast_to(FA[x + 1, 4 * j + k : 4 * j + k + 1, :], (8, 128)) for k in range(4)]
            FX2[x, 8 * j : 8 * j + 8, :] = jnp.where(
                sub < 4, jnp.where(sub < 2, rows[0], rows[1]), jnp.where(sub < 6, rows[2], rows[3])
            )

    def weights2(x, carry):
        for c in range(3):
            out = pl.ds(8 * c, 8)
            f = FX2[x + 1, 8 * c + 8 : 8 * c + 16, :]
            inside = f > 0.0
            rf = 1.0 / jnp.where(inside, f, 1.0)
            ryp = FX2[x + 1, pl.ds(8 * c + 9, 8), :] * rf
            rym = FX2[x + 1, pl.ds(8 * c + 7, 8), :] * rf
            AYP2[x, out, :] = 1.0 + ryp
            AYM2[x, out, :] = 1.0 + rym
            RF2[x, out, :] = 32.0 * rf
            HF2[x, out, :] = 0.03125 * f
            ry = 4.0 + ryp + rym
            for r in range(2):
                rp = FX2[x + 2, 8 * c + 8 : 8 * c + 16, :] * rf if r == 1 else jnp.ones_like(rf)
                rm = FX2[x, 8 * c + 8 : 8 * c + 16, :] * rf if r == 0 else jnp.ones_like(rf)
                AXP2[2 * x + r, out, :] = 1.0 + rp
                AXM2[2 * x + r, out, :] = 1.0 + rm
                a = ry + rp + rm
                A2[2 * x + r, out, :] = a
                INV2[2 * x + r, out, :] = jnp.where(inside, OMEGA / (a + BS[2]), 0.0)
        return carry

    lax.fori_loop(0, 8, weights2, 0)
    for ref in (B2, V2, W2):
        for x in (0, 1, 18, 19):
            for c in range(3):
                ref[x, 8 * c : 8 * c + 8, :] = zero

    for copy in first1:
        copy.wait_recv()

    def start1(q, carry):
        t = (q + 3) // 4
        for c in range(4):
            rows = pl.ds(8 * c, 8)
            B1[q, rows, :] = F1[q, rows, :] * INV1[q, rows, :] * (RF1[t, rows, :] * RPS[1])
        return carry

    def spread1(v_ref, q, row):
        t = (q + 3) // 4
        rows = pl.ds(row, 8)
        centre = v_ref[q, rows, :]
        total = (
            AXP1[q, rows, :] * v_ref[q + 1, rows, :]
            + AXM1[q, rows, :] * v_ref[q - 1, rows, :]
            + AYP1[t, rows, :] * v_ref[q, pl.ds(row + 1, 8), :]
            + AYM1[t, rows, :] * v_ref[q, pl.ds(row - 1, 8), :]
            + BU[1] * zup(centre, 1)
            + BD[1] * zdn(centre, 1)
        )
        return centre, total

    def relax1(src, dst, fresh):
        def body(q, carry):
            for c in range(3):
                rows = pl.ds(8 * c + 4, 8)
                centre, total = spread1(src, q, 8 * c + 4)
                kept = (1.0 + KEEP) * centre if fresh else KEEP * centre + B1[q, rows, :]
                dst[q, rows, :] = kept + INV1[q, rows, :] * total
            return carry

        return body

    lax.fori_loop(3, 15, start1, 0)
    lax.fori_loop(4, 14, relax1(B1, V1, True), 0)

    def down1(i, carry):
        for c in range(2):
            rows = pl.ds(8 * c + 8, 8)
            left = []
            for q in (2 * i + 5, 2 * i + 6):
                centre, total = spread1(V1, q, 8 * c + 8)
                hp = HF1[(q + 3) // 4, rows, :] * permits[1]
                left.append(F1[q, rows, :] - hp * ((A1[q, rows, :] + BS[1]) * centre - total))
            T1[i, pl.ds(8 * c, 8), :] = pair(left[0] + left[1], 2)
        F2[4 * g + i, 8:16, :] = 0.125 * (
            T1[i, pl.ds(0, 8, stride=2), :] + T1[i, pl.ds(1, 8, stride=2), :]
        )
        return carry

    lax.fori_loop(0, 4, down1, 0)
    for copy in first2 + late1:
        copy.start()

    tiles = devs + 2

    def yup(v, after, level):
        if level == 5:
            return after
        step = 1 << (level - 2)
        return jnp.where((lane & 6) >= 8 - step, roll(after, 8 - step), roll(v, -step))

    def ydn(v, before, level):
        if level == 5:
            return before
        step = 1 << (level - 2)
        return jnp.where((lane & 6) < step, roll(before, step - 8), roll(v, step))

    for k in range(3):
        for ref in (FC, VC, WC, BC):
            ref[k, 0, :, :] = zero
            ref[k, tiles - 1, :, :] = zero
    for e in range(devs):
        cols = [jnp.broadcast_to(fills[:, 4 * e + k : 4 * e + k + 1], (8, 128)) for k in range(4)]
        low, high = (lane & 2) == 0, (lane & 4) == 0
        f = jnp.where(high, jnp.where(low, cols[0], cols[1]), jnp.where(low, cols[2], cols[3]))
        FC[0, e + 1, :, :] = f
        f = 0.25 * pair(spair(f, 1), 2)
        FC[1, e + 1, :, :] = f
        FC[2, e + 1, :, :] = 0.25 * pair(spair(f, 2), 4)

    def weights_coarse(e, carry):
        for k in range(3):
            level = k + 3
            step = 1 << k
            f = FC[k, e, :, :]
            rf = 1.0 / f
            ryp = yup(f, FC[k, e + 1, :, :], level) * rf
            rym = ydn(f, FC[k, e - 1, :, :], level) * rf
            last, first = sub >= 8 - step, sub < step
            rxp = jnp.where(last, 0.0, sroll(f, -step) * rf)
            rxm = jnp.where(first, 0.0, sroll(f, step) * rf)
            AXPC[k, e, :, :] = jnp.where(last, 0.0, 1.0 + rxp)
            AXMC[k, e, :, :] = jnp.where(first, 0.0, 1.0 + rxm)
            AYPC[k, e, :, :] = 1.0 + ryp
            AYMC[k, e, :, :] = 1.0 + rym
            a = 4.0 + ryp + rym + rxp + rxm
            AC[k, e, :, :] = a
            INVC[k, e, :, :] = OMEGA / (a + BS[level])
        return carry

    lax.fori_loop(1, devs + 1, weights_coarse, 0)

    for copy in first2:
        copy.wait_recv()

    def start2(q, carry):
        for c in range(3):
            rows = pl.ds(8 * c, 8)
            B2[q + 2, rows, :] = F2[q, rows, :] * INV2[q, rows, :] * (RF2[q // 2, rows, :] * RPS[2])
        return carry

    def spread2(v_ref, q, row):
        rows = pl.ds(row, 8)
        centre = v_ref[q + 2, rows, :]
        total = (
            AXP2[q, rows, :] * v_ref[q + 3, rows, :]
            + AXM2[q, rows, :] * v_ref[q + 1, rows, :]
            + AYP2[q // 2, rows, :] * v_ref[q + 2, pl.ds(row + 1, 8), :]
            + AYM2[q // 2, rows, :] * v_ref[q + 2, pl.ds(row - 1, 8), :]
            + BU[2] * zup(centre, 2)
            + BD[2] * zdn(centre, 2)
        )
        return centre, total

    def relax2(src, dst, fresh):
        def body(q, carry):
            for c in range(2):
                rows = pl.ds(8 * c + 4, 8)
                centre, total = spread2(src, q, 8 * c + 4)
                kept = (1.0 + KEEP) * centre if fresh else KEEP * centre + B2[q + 2, rows, :]
                dst[q + 2, rows, :] = kept + INV2[q, rows, :] * total
            return carry

        return body

    lax.fori_loop(0, 16, start2, 0)
    lax.fori_loop(0, 16, relax2(B2, V2, True), 0)
    packed = zero
    for x in range(8):
        left = []
        for q in (2 * x, 2 * x + 1):
            centre, total = spread2(V2, q, 8)
            hp = HF2[x, 8:16, :] * permits[2]
            left.append(F2[q, 8:16, :] - hp * ((A2[q, 8:16, :] + BS[2]) * centre - total))
        both = pair(left[0] + left[1], 4)
        both = jnp.where((sub & 6) == (lane & 6), both, 0.0)
        packed = jnp.where(sub == x, jnp.sum(both, axis=0, keepdims=True), packed)
    G[pl.ds(d, 1), :, :] = (0.125 * packed)[None]

    def tell(k, carry):
        pltpu.make_async_remote_copy(
            src_ref=G.at[d],
            dst_ref=G.at[d],
            send_sem=s3_send,
            recv_sem=s3_recv,
            device_id=(g, lax.rem(d + k, devs)),
            device_id_type=MESH,
        ).start()
        return carry

    lax.fori_loop(1, devs, tell, 0)

    for copy in late0:
        copy.wait_recv()
    for q in (0, 1, 22, 23):
        start0(q, 0)
    for q in (1, 2, 21, 22):
        relax0(B0, V0, True)(q, 0)
    for copy in late1:
        copy.wait_recv()
    for q in (0, 1, 2, 15, 16, 17):
        start1(q, 0)
    for q in (1, 2, 3, 14, 15, 16):
        relax1(B1, V1, True)(q, 0)

    everyone = pltpu.make_async_copy(G.at[0 : devs - 1], G.at[0 : devs - 1], s3_recv)
    everyone.wait()

    def spread_coarse(k, v_ref, e):
        level = k + 3
        step = 1 << k
        centre = v_ref[k, e, :, :]
        total = (
            AXPC[k, e, :, :] * sroll(centre, -step)
            + AXMC[k, e, :, :] * sroll(centre, step)
            + AYPC[k, e, :, :] * yup(centre, v_ref[k, e + 1, :, :], level)
            + AYMC[k, e, :, :] * ydn(centre, v_ref[k, e - 1, :, :], level)
            + BU[level] * zup(centre, level)
            + BD[level] * zdn(centre, level)
        )
        return centre, total

    per = 8 if devs % 8 == 0 else 4

    def over_tiles(body):
        def several(i, carry):
            for j in range(per):
                body(i * per + j + 1)
            return carry

        lax.fori_loop(0, devs // per, several, 0)

    def start_coarse(k, f_ref):
        factor = 2.0 * 4.0 ** (k + 3)

        def body(e):
            f = f_ref[e - 1, :, :]
            BC[k, e, :, :] = f * INVC[k, e, :, :] * (factor * RPS[k + 3]) / FC[k, e, :, :]

        over_tiles(body)

    def relax_coarse(k, src, dst, fresh=False):
        def body(e):
            centre, total = spread_coarse(k, src, e)
            kept = (1.0 + KEEP) * centre if fresh else KEEP * centre + BC[k, e, :, :]
            dst[k, e, :, :] = kept + INVC[k, e, :, :] * total

        over_tiles(body)

    def down_coarse(k, f_ref, next_ref):
        level = k + 3
        factor = 0.5 * 0.25**level

        def body(e):
            centre, total = spread_coarse(k, VC, e)
            hp = FC[k, e, :, :] * (factor * permits[level])
            left = f_ref[e - 1, :, :] - hp * ((AC[k, e, :, :] + BS[level]) * centre - total)
            left = pair(pair(spair(left, 1 << k), 1 << (k + 1)), 1 << level)
            next_ref[e - 1, :, :] = 0.125 * left

        over_tiles(body)

    for k, f_ref, next_ref in ((0, G, F4), (1, F4, F5)):
        start_coarse(k, f_ref)
        relax_coarse(k, BC, VC, fresh=True)
        down_coarse(k, f_ref, next_ref)
    start_coarse(2, F5)
    relax_coarse(2, BC, VC, fresh=True)

    def two_sweeps(i, carry):
        relax_coarse(2, VC, WC)
        relax_coarse(2, WC, VC)
        return carry

    lax.fori_loop(0, (SWEEPS - 2) // 2, two_sweeps, 0)
    for k in (1, 0):

        def correct(e):
            VC[k, e, :, :] = VC[k, e, :, :] + VC[k + 1, e, :, :]

        over_tiles(correct)
        relax_coarse(k, VC, WC)
        relax_coarse(k, WC, VC)

    yl = (lane >> 1) & 3
    for b in range(3):
        tile = VC[0, d + b, :, :]
        rolled = {s: (tile if s == 0 else roll(tile, -2 * s)) for s in range(-3, 4)}
        for k in range(4):
            UU[b, k, :, :] = jnp.where(
                yl < 2,
                jnp.where(yl == 0, rolled[k], rolled[k - 1]),
                jnp.where(yl == 2, rolled[k - 2], rolled[k - 3]),
            )
    for x in range(8):
        for b in range(3):
            rows = [jnp.broadcast_to(UU[b, k, x : x + 1, :], (8, 128)) for k in range(4)]
            fine = jnp.where(
                sub < 4, jnp.where(sub < 2, rows[0], rows[1]), jnp.where(sub < 6, rows[2], rows[3])
            )
            for q in (2 * x + 2, 2 * x + 3):
                V2[q, 8 * b : 8 * b + 8, :] = V2[q, 8 * b : 8 * b + 8, :] + fine
    lax.fori_loop(0, 16, relax2(V2, W2, False), 0)
    lax.fori_loop(0, 16, relax2(W2, V2, False), 0)

    def raise1(i, carry):
        for row, count in ((6, 8), (14, 4)):
            fine = V2[4 * g + i, pl.ds(row, count), :]
            for odd in range(2):
                P1[i, pl.ds(2 * (row - 6) + odd, count, stride=2), :] = fine
        for q in (2 * i + 1, 2 * i + 2):
            for c in range(3):
                rows = pl.ds(8 * c + 4, 8)
                V1[q, rows, :] = V1[q, rows, :] + P1[i, 8 * c : 8 * c + 8, :]
        return carry

    lax.fori_loop(0, 8, raise1, 0)
    lax.fori_loop(2, 16, relax1(V1, W1, False), 0)
    lax.fori_loop(3, 15, relax1(W1, V1, False), 0)

    def raise0(i, carry):
        for row, count in ((6, 8), (14, 8), (22, 4)):
            coarse = V1[i + 3, pl.ds(row, 8), :]
            fine = (jnp.where(even, coarse, roll(coarse, 1)), jnp.where(even, roll(coarse, -1), coarse))
            for h in range(2):
                for odd in range(2):
                    P0[h, i, pl.ds(2 * (row - 6) + odd, count, stride=2), :] = fine[h][0:count, :]
        for q in (2 * i, 2 * i + 1):
            for h in range(2):
                for c in range(5):
                    rows = pl.ds(8 * c + 8, 8)
                    V0[h, q, rows, :] = V0[h, q, rows, :] + P0[h, i, 8 * c : 8 * c + 8, :]
        return carry

    lax.fori_loop(0, 12, raise0, 0)
    lax.fori_loop(2, 22, relax0(V0, W0, False), 0)
    lax.fori_loop(3, 21, relax0(W0, V0, False), 0)

    def finish(x, carry):
        for c in range(4):
            centre, left = left0(V0, x + 4, c)
            for h in range(2):
                pot_ref[x, 8 * c : 8 * c + 8, h * 128 : h * 128 + 128] = centre[h]
                res_ref[x, 8 * c : 8 * c + 8, h * 128 : h * 128 + 128] = left[h]
        return carry

    lax.fori_loop(0, 16, finish, 0)

    for copy in first0 + late0 + first1 + late1 + first2:
        copy.wait_send()
    pltpu.make_async_copy(G.at[0 : devs - 1], G.at[0 : devs - 1], s3_send).wait()


def solution(mesh):
    groups, devs = mesh.shape["group"], mesh.shape["dev"]

    def rows(*shape):
        return pltpu.VMEM(shape + (128,), jnp.float32)

    def sems(count):
        return pltpu.SemaphoreType.DMA((count,))

    def on_device(source, plane_layer, layer_permittivity, tile_kind, kind_fill):
        vmem = pl.BlockSpec(memory_space=pltpu.VMEM)
        smem = pl.BlockSpec(memory_space=pltpu.SMEM)
        tiles = devs + 2
        coarse = rows(3, tiles, 8)
        out = jax.ShapeDtypeStruct(source.shape, jnp.float32)
        scratch = [
            rows(2, 24, 48), rows(2, 24, 56), rows(2, 24, 56), rows(2, 24, 56),
            rows(2, 12, 40), rows(12, 40), rows(12, 40), rows(12, 40),
            rows(4, 40), rows(4, 40), rows(4, 40), rows(4, 40), rows(6, 64),
            rows(8, 32), rows(2, 12, 40),
            rows(18, 32), rows(18, 32), rows(18, 32), rows(18, 32),
            rows(18, 32), rows(18, 32), rows(18, 32), rows(18, 32),
            rows(6, 32), rows(6, 32), rows(6, 32), rows(6, 32), rows(6, 48),
            rows(4, 16), rows(8, 24),
            rows(16, 24), rows(20, 24), rows(20, 24), rows(20, 24),
            rows(16, 24), rows(16, 24), rows(16, 24), rows(16, 24),
            rows(8, 24), rows(8, 24), rows(8, 24), rows(8, 24), rows(10, 40),
            rows(3, 4, 8),
            rows(12, 24), rows(devs, 8), rows(devs, 8), rows(devs, 8),
            coarse, coarse, coarse, coarse, coarse, coarse, coarse, coarse, coarse, coarse,
            sems(2), sems(18), sems(18), sems(18), sems(18), sems(9), sems(9), sems(9), sems(9),
            sems(3 * groups - 1), sems(3 * groups - 1),
            pltpu.SemaphoreType.DMA, pltpu.SemaphoreType.DMA,
        ]
        return pl.pallas_call(
            functools.partial(kernel, groups, devs),
            out_shape=(out, out),
            in_specs=[vmem, vmem, smem, smem, pl.BlockSpec(memory_space=pl.ANY)],
            out_specs=(vmem, vmem),
            scratch_shapes=scratch,
            compiler_params=pltpu.CompilerParams(
                collective_id=0, has_side_effects=True, vmem_limit_bytes=48 * 1024 * 1024
            ),
        )(plane_layer.reshape(2, 128), tile_kind, layer_permittivity, kind_fill, source)

    in_specs = (P("group", "dev", None), P(), P(), P(), P())
    out_specs = (P("group", "dev", None), P("group", "dev", None))
    return jax.shard_map(
        on_device, mesh=mesh, in_specs=in_specs, out_specs=out_specs, check_vma=False
    )
```

```python
import functools

import jax
import jax.numpy as jnp
from jax import lax
from jax.experimental import pallas as pl
from jax.experimental.pallas import tpu as pltpu
from jax.sharding import PartitionSpec as P

MESH = pl.DeviceIdType.MESH
OMEGA = 2.0 / 3.0
KEEP = 1.0 - OMEGA
SWEEPS = 24
NEIGHBOURS = tuple(
    (dx, dy) for dx in (-1, 0, 1) for dy in (-1, 0, 1) if (dx, dy) != (0, 0)
)


def kernel(
    groups,
    devs,
    layers_hbm,
    kinds_hbm,
    permit_hbm,
    fill_hbm,
    source,
    pot_ref,
    res_ref,
    layers_ref, kinds_ref, permit_ref, fill_ref,
    F0, V0, W0, B0, INV0, A0, AXP0, AXM0, AYP0, AYM0, RF0, HF0, FX0, T0, P0,
    F1, V1, W1, B1, INV1, A1, AXP1, AXM1, AYP1, AYM1, RF1, HF1, FX1, T1, P1,
    F2, V2, W2, B2, INV2, A2, AXP2, AXM2, AYP2, AYM2, RF2, HF2, FX2, UU,
    FA, G, F3, F4, F5, FC, VC, WC, BC, INVC, AC, AXPC, AXMC, AYPC, AYMC,
    input_sem, local_sem, s0_send, s0_recv, s0l_send, s0l_recv, s1_send, s1_recv, s1l_send, s1l_recv,
    s2_send, s2_recv, s3_send, s3_recv,
):
    g = lax.axis_index("group")
    d = lax.axis_index("dev")
    f32 = jnp.float32
    lane = lax.broadcasted_iota(jnp.int32, (8, 128), 1)
    sub = lax.broadcasted_iota(jnp.int32, (8, 128), 0)
    even = (lane & 1) == 0
    zero = jnp.zeros((8, 128), f32)
    blocks = devs // 4
    counts = (4 * blocks, 2 * blocks, blocks)

    def peer(dx, dy):
        return (lax.rem(g + dx + groups, groups), lax.rem(d + dy + devs, devs))

    def roll(v, shift):
        return pltpu.roll(v, shift % 128, 1)

    def sroll(v, shift):
        return pltpu.roll(v, shift % 8, 0)

    def permute(v, index):
        return jnp.take_along_axis(v, index, axis=1, mode="promise_in_bounds")

    barrier = pltpu.get_barrier_semaphore()
    column = [(dx, dy) for dx in range(groups) for dy in (-1, 0, 1) if (dx, dy) != (0, 0)]
    for dx, dy in column:
        pl.semaphore_signal(barrier, inc=1, device_id=peer(dx, dy), device_id_type=MESH)

    def greet(k, carry):
        pl.semaphore_signal(barrier, inc=1, device_id=(g, lax.rem(d + k, devs)), device_id_type=MESH)
        return carry

    inputs = [
        pltpu.make_async_copy(src, dst, input_sem.at[i])
        for i, (src, dst) in enumerate(
            (
                (layers_hbm, layers_ref),
                (kinds_hbm, kinds_ref),
                (permit_hbm, permit_ref),
                (fill_hbm, fill_ref),
            )
        )
    ]
    own = [
        pltpu.make_async_copy(
            source.at[:, :, h * 128 : h * 128 + 128], F0.at[h, 4:20, 8:40, :], local_sem.at[h]
        )
        for h in range(2)
    ]
    for copy in inputs:
        copy.start()
    lax.fori_loop(2, devs - 1, greet, 0)
    for copy in own:
        copy.start()

    def halo0(dx, dy, h, late):
        px = {0: (0, 16, 4), 1: (14, 2, 2), -1: (0, 2, 20)}[dx]
        if late:
            px = {1: (12, 2, 0), -1: (2, 2, 22)}[dx]
        py = {0: (0, 32, 8), 1: (24, 8, 0), -1: (0, 8, 40)}[dy]
        slot = ((dx + 1) * 3 + dy + 1) * 2 + h
        send, recv = (s0l_send, s0l_recv) if late else (s0_send, s0_recv)
        return pltpu.make_async_remote_copy(
            src_ref=source.at[px[0] : px[0] + px[1], py[0] : py[0] + py[1], h * 128 : h * 128 + 128],
            dst_ref=F0.at[h, px[2] : px[2] + px[1], py[2] : py[2] + py[1], :],
            send_sem=send.at[slot],
            recv_sem=recv.at[slot],
            device_id=peer(dx, dy),
            device_id_type=MESH,
        )

    first0 = [halo0(dx, dy, h, False) for dx, dy in NEIGHBOURS for h in range(2)]
    late0 = [halo0(dx, dy, h, True) for dx, dy in NEIGHBOURS if dx for h in range(2)]

    def halo1(dx, dy, late):
        px = {0: (0, 8, 5), 1: (6, 2, 3), -1: (0, 2, 13)}[dx]
        if late:
            px = {1: (3, 3, 0), -1: (2, 3, 15)}[dx]
        py = {0: (0, 16, 8), 1: (8, 8, 0), -1: (0, 8, 24)}[dy]
        slot = (dx + 1) * 3 + dy + 1
        send, recv = (s1l_send, s1l_recv) if late else (s1_send, s1_recv)
        return pltpu.make_async_remote_copy(
            src_ref=F1.at[px[0] + 5 : px[0] + px[1] + 5, py[0] + 8 : py[0] + py[1] + 8, :],
            dst_ref=F1.at[px[2] : px[2] + px[1], py[2] : py[2] + py[1], :],
            send_sem=send.at[slot],
            recv_sem=recv.at[slot],
            device_id=peer(dx, dy),
            device_id_type=MESH,
        )

    first1 = [halo1(dx, dy, False) for dx, dy in NEIGHBOURS]
    late1 = [halo1(dx, dy, True) for dx, dy in NEIGHBOURS if dx]

    def block2(slot):
        dx, dy = column[slot]
        return pltpu.make_async_remote_copy(
            src_ref=F2.at[pl.ds(4 * g, 4), 8:16, :],
            dst_ref=F2.at[pl.ds(4 * g, 4), 8 - 8 * dy : 16 - 8 * dy, :],
            send_sem=s2_send.at[slot],
            recv_sem=s2_recv.at[slot],
            device_id=peer(dx, dy),
            device_id_type=MESH,
        )

    first2 = [block2(slot) for slot in range(len(column))]

    for copy in inputs:
        copy.wait()
    kinds = kinds_ref[...]
    fills = zero
    for kind in range(fill_ref.shape[0]):
        fills = jnp.where(kinds == kind, fill_ref[kind], fills)
    fills = jnp.where(lane < 4 * devs, fills, 0.0)
    shifted = pltpu.roll(fills, lax.rem(8 + 128 - 4 * d + 128, 128), 1)
    tile_y = 4 * d - 8 + lane
    shifted = jnp.where((tile_y >= 0) & (tile_y < 4 * devs), shifted, 0.0)
    for c in range(3):
        for x in (0, 1, 10, 11):
            FA[x, 8 * c : 8 * c + 8, :] = zero
        for x in range(8):
            row = jnp.broadcast_to(shifted[x : x + 1, :], (8, 128))
            picked = jnp.sum(jnp.where(lane == sub + 8 * c, row, 0.0), axis=1, keepdims=True)
            FA[x + 2, 8 * c : 8 * c + 8, :] = jnp.broadcast_to(picked, (8, 128))

    permit0 = []
    for h in range(2):
        layer = jnp.broadcast_to(layers_ref[h : h + 1, :], (8, 128))
        value = zero
        for k in range(permit_ref.shape[0]):
            value = jnp.where(layer == k, permit_ref[k], value)
        permit0.append(value)

    def zup0(h0, h1):
        r0, r1 = roll(h0, -1), roll(h1, -1)
        return jnp.where(lane == 127, r1, r0), r1

    def zdn0(h0, h1):
        r0, r1 = roll(h0, 1), roll(h1, 1)
        return r0, jnp.where(lane == 0, r0, r1)

    def zup(v, level):
        return roll(v, -(1 << (level - 1)))

    def zdn(v, level):
        return roll(v, 1 << (level - 1))

    def pair(v, step):
        return v + jnp.where((lane & step) == 0, roll(v, -step), roll(v, step))

    def spair(v, step):
        return v + jnp.where((sub & step) == 0, sroll(v, -step), sroll(v, step))

    gather_z = jnp.where(lane < 64, 2 * lane, 2 * lane - 127)
    low_z = lane >> 1
    high_z = low_z + 64

    def halves(h0, h1):
        both = jnp.where(even, h0, h1) + jnp.where(even, roll(h0, -1), roll(h1, 1))
        return permute(both, gather_z)

    pu0, pu1 = zup0(*permit0)
    pd0, pd1 = zdn0(*permit0)
    RP0 = [1.0 / p for p in permit0]
    ru = [pu0 * RP0[0], jnp.where(lane == 127, 0.0, pu1 * RP0[1])]
    rd = [jnp.where(lane == 0, 0.0, pd0 * RP0[0]), pd1 * RP0[1]]
    BU0 = [0.5 + 0.5 * ru[0], jnp.where(lane == 127, 0.0, 0.5 + 0.5 * ru[1])]
    BD0 = [jnp.where(lane == 0, 0.0, 0.5 + 0.5 * rd[0]), 0.5 + 0.5 * rd[1]]
    BS0 = [1.0 + 0.5 * (ru[h] + rd[h]) for h in range(2)]
    permits = [None, 0.5 * halves(*permit0)]
    for level in (2, 3, 4, 5):
        permits.append(0.5 * pair(permits[level - 1], 1 << (level - 2)))
    RPS, BU, BD, BS = [None], [None], [None], [None]
    for level in range(1, 6):
        p = permits[level]
        step = 1 << (level - 1)
        rp = 1.0 / p
        top, bottom = lane >= 128 - step, lane < step
        up = jnp.where(top, 0.0, zup(p, level) * rp)
        dn = jnp.where(bottom, 0.0, zdn(p, level) * rp)
        RPS.append(rp)
        BU.append(jnp.where(top, 0.0, 0.5 + 0.5 * up))
        BD.append(jnp.where(bottom, 0.0, 0.5 + 0.5 * dn))
        BS.append(1.0 + 0.5 * (up + dn))

    for t in range(6):
        for j in range(8):
            FX0[t, 8 * j : 8 * j + 8, :] = jnp.broadcast_to(FA[2 * g + t, 6 + j : 7 + j, :], (8, 128))

    def half(ratio):
        return 0.5 + 0.5 * ratio

    for c in range(5):
        at = 8 * c
        out = pl.ds(at, 8)
        for t in range(4):
            f = FX0[t + 1, pl.ds(at + 12, 8), :]
            inside = f > 0.0
            rf = 1.0 / jnp.where(inside, f, 1.0)
            ayp = half(FX0[t + 1, pl.ds(at + 13, 8), :] * rf)
            aym = half(FX0[t + 1, pl.ds(at + 11, 8), :] * rf)
            axp = half(FX0[t + 2, pl.ds(at + 12, 8), :] * rf)
            axm = half(FX0[t, pl.ds(at + 12, 8), :] * rf)
            AYP0[t, out, :] = ayp
            AYM0[t, out, :] = aym
            AXP0[t, out, :] = axp
            AXM0[t, out, :] = axm
            RF0[t, out, :] = rf
            HF0[t, out, :] = f
            for kind in range(3):
                if (t, kind) in ((0, 0), (3, 2)):
                    continue
                a = ayp + aym + (axp if kind == 2 else 1.0) + (axm if kind == 0 else 1.0)
                A0[3 * t + kind, out, :] = a
                for h in range(2):
                    INV0[h, 3 * t + kind, out, :] = jnp.where(inside, OMEGA / (a + BS0[h]), 0.0)

    pl.semaphore_wait(barrier, len(column) + devs - 3)
    for copy in first0:
        copy.start()

    for t in range(6):
        for j in range(6):
            FX1[t, 8 * j : 8 * j + 8, :] = jnp.where(
                sub < 4,
                jnp.broadcast_to(FA[2 * g + t, 4 + 2 * j : 5 + 2 * j, :], (8, 128)),
                jnp.broadcast_to(FA[2 * g + t, 5 + 2 * j : 6 + 2 * j, :], (8, 128)),
            )

    def weights1(c, carry):
        at = pl.multiple_of(8 * c, 8)
        out = pl.ds(at, 8)
        for t in range(6):
            f = FX1[t, pl.ds(at + 8, 8), :]
            inside = f > 0.0
            rf = 1.0 / jnp.where(inside, f, 1.0)
            ayp = half(FX1[t, pl.ds(at + 9, 8), :] * rf)
            aym = half(FX1[t, pl.ds(at + 7, 8), :] * rf)
            AYP1[t, out, :] = ayp
            AYM1[t, out, :] = aym
            RF1[t, out, :] = 4.0 * rf
            HF1[t, out, :] = 0.25 * f
            ay = ayp + aym
            axp = half(FX1[t + 1, pl.ds(at + 8, 8), :] * rf) if t < 5 else None
            axm = half(FX1[t - 1, pl.ds(at + 8, 8), :] * rf) if t > 0 else None
            if t < 5:
                AXP1[t, out, :] = axp
            if t > 0:
                AXM1[t, out, :] = axm
            for r in range(4):
                q = 4 * t + r - 3
                if q < 0 or q > 17 or r == 2:
                    continue
                a = ay + (axp if r == 3 else 1.0) + (axm if r == 0 else 1.0)
                A1[3 * t + min(r, 2), out, :] = a
                INV1[3 * t + min(r, 2), out, :] = jnp.where(inside, OMEGA / (a + BS[1]), 0.0)
        return carry

    lax.fori_loop(0, 4, weights1, 0)

    for x in range(10):
        for j in range(5):
            rows = [jnp.broadcast_to(FA[x + 1, 4 * j + k : 4 * j + k + 1, :], (8, 128)) for k in range(4)]
            FX2[x, 8 * j : 8 * j + 8, :] = jnp.where(
                sub < 4, jnp.where(sub < 2, rows[0], rows[1]), jnp.where(sub < 6, rows[2], rows[3])
            )

    def weights2(x, carry):
        for c in range(3):
            out = pl.ds(8 * c, 8)
            f = FX2[x + 1, 8 * c + 8 : 8 * c + 16, :]
            inside = f > 0.0
            rf = 1.0 / jnp.where(inside, f, 1.0)
            ayp = half(FX2[x + 1, pl.ds(8 * c + 9, 8), :] * rf)
            aym = half(FX2[x + 1, pl.ds(8 * c + 7, 8), :] * rf)
            axp = half(FX2[x + 2, 8 * c + 8 : 8 * c + 16, :] * rf)
            axm = half(FX2[x, 8 * c + 8 : 8 * c + 16, :] * rf)
            AYP2[x, out, :] = ayp
            AYM2[x, out, :] = aym
            AXP2[x, out, :] = axp
            AXM2[x, out, :] = axm
            RF2[x, out, :] = 16.0 * rf
            HF2[x, out, :] = 0.0625 * f
            for r in range(2):
                a = ayp + aym + (axp if r == 1 else axm) + 1.0
                A2[2 * x + r, out, :] = a
                INV2[2 * x + r, out, :] = jnp.where(inside, OMEGA / (a + BS[2]), 0.0)
        return carry

    lax.fori_loop(0, 8, weights2, 0)
    for ref in (B2, V2, W2):
        for x in (0, 1, 18, 19):
            for c in range(3):
                ref[x, 8 * c : 8 * c + 8, :] = zero

    def kind0(q):
        t, r = (q + 4) // 8, (q + 4) % 8
        kind = 0 if r == 0 else 2 if r == 7 else 1
        return t, kind, 3 * t + kind

    def start0(q, y, count):
        t, _, cls = kind0(q)
        w = pl.ds(y + 4, count)
        rf = RF0[t, w, :]
        for h in range(2):
            f = F0[h, q, pl.ds(y + 8, count), :]
            B0[h, q, pl.ds(y + 12, count), :] = f * INV0[h, cls, w, :] * (rf * RP0[h][0:count, :])

    def weighted(weight, v):
        return v if weight is None else weight * v

    def spread0(v_ref, q, y):
        t, kind, _ = kind0(q)
        w = pl.ds(y + 4, 8)
        axp = AXP0[t, w, :] if kind == 2 else None
        axm = AXM0[t, w, :] if kind == 0 else None
        ayp, aym = AYP0[t, w, :], AYM0[t, w, :]
        centre = [v_ref[h, q, pl.ds(y + 12, 8), :] for h in range(2)]
        up, dn = zup0(*centre), zdn0(*centre)
        total = []
        for h in range(2):
            total.append(
                weighted(axp, v_ref[h, q + 1, pl.ds(y + 12, 8), :])
                + weighted(axm, v_ref[h, q - 1, pl.ds(y + 12, 8), :])
                + ayp * v_ref[h, q, pl.ds(y + 13, 8), :]
                + aym * v_ref[h, q, pl.ds(y + 11, 8), :]
                + BU0[h] * up[h]
                + BD0[h] * dn[h]
            )
        return centre, total

    def relax0(src, dst, fresh, q, c):
        cls = kind0(q)[2]
        y = 8 * c - 4
        centre, total = spread0(src, q, y)
        for h in range(2):
            if fresh:
                kept = (1.0 + KEEP) * centre[h]
            else:
                kept = KEEP * centre[h] + B0[h, q, pl.ds(y + 12, 8), :]
            dst[h, q, pl.ds(y + 12, 8), :] = kept + INV0[h, cls, pl.ds(y + 4, 8), :] * total[h]

    def left0(v_ref, q, c):
        t, _, cls = kind0(q)
        centre, total = spread0(v_ref, q, 8 * c)
        a = A0[cls, pl.ds(8 * c + 4, 8), :]
        hf = HF0[t, pl.ds(8 * c + 4, 8), :]
        left = []
        for h in range(2):
            f = F0[h, q, pl.ds(8 * c + 8, 8), :]
            left.append(f - hf * permit0[h] * ((a + BS0[h]) * centre[h] - total[h]))
        return centre, left

    for copy in own:
        copy.wait()
    for q in range(4, 20):
        for c in range(4):
            start0(q, 8 * c, 8)
    for q in range(5, 19):
        for c in range(1, 4):
            relax0(B0, V0, True, q, c)
    for copy in first0:
        copy.wait_recv()
    for q in range(2, 22):
        if 4 <= q < 20:
            start0(q, -4, 4)
            start0(q, 32, 4)
        else:
            for c in range(5):
                start0(q, 8 * c - 4, 8)
    for q in range(3, 21):
        for c in (0, 4) if 5 <= q < 19 else range(5):
            relax0(B0, V0, True, q, c)

    for i in range(8):
        for c in range(4):
            first = left0(V0, 2 * i + 4, c)[1]
            second = left0(V0, 2 * i + 5, c)[1]
            for h in range(2):
                T0[i, h, pl.ds(8 * c, 8), :] = first[h] + second[h]
        for c in range(2):
            both = [
                T0[i, h, pl.ds(16 * c, 8, stride=2), :] + T0[i, h, pl.ds(16 * c + 1, 8, stride=2), :]
                for h in range(2)
            ]
            F1[i + 5, 8 * c + 8 : 8 * c + 16, :] = 0.125 * halves(*both)
    for copy in first1 + late0:
        copy.start()

    for copy in first1:
        copy.wait_recv()

    def kind1(q):
        t, r = (q + 3) // 4, (q + 3) % 4
        return t, r, 3 * t + (0, 1, 1, 2)[r]

    def start1(q):
        t, _, cls = kind1(q)
        for c in range(4):
            rows = pl.ds(8 * c, 8)
            B1[q, rows, :] = F1[q, rows, :] * INV1[cls, rows, :] * (RF1[t, rows, :] * RPS[1])

    def spread1(v_ref, q, row):
        t, r, _ = kind1(q)
        rows = pl.ds(row, 8)
        axp = AXP1[t, rows, :] if r == 3 else None
        axm = AXM1[t, rows, :] if r == 0 else None
        centre = v_ref[q, rows, :]
        total = (
            weighted(axp, v_ref[q + 1, rows, :])
            + weighted(axm, v_ref[q - 1, rows, :])
            + AYP1[t, rows, :] * v_ref[q, pl.ds(row + 1, 8), :]
            + AYM1[t, rows, :] * v_ref[q, pl.ds(row - 1, 8), :]
            + BU[1] * zup(centre, 1)
            + BD[1] * zdn(centre, 1)
        )
        return centre, total

    def relax1(src, dst, fresh, q):
        cls = kind1(q)[2]
        for c in range(3):
            rows = pl.ds(8 * c + 4, 8)
            centre, total = spread1(src, q, 8 * c + 4)
            kept = (1.0 + KEEP) * centre if fresh else KEEP * centre + B1[q, rows, :]
            dst[q, rows, :] = kept + INV1[cls, rows, :] * total

    for q in range(3, 15):
        start1(q)
    for q in range(4, 14):
        relax1(B1, V1, True, q)
    for i in range(4):
        for c in range(2):
            rows = pl.ds(8 * c + 8, 8)
            left = []
            for q in (2 * i + 5, 2 * i + 6):
                t, _, cls = kind1(q)
                centre, total = spread1(V1, q, 8 * c + 8)
                hp = HF1[t, rows, :] * permits[1]
                left.append(F1[q, rows, :] - hp * ((A1[cls, rows, :] + BS[1]) * centre - total))
            T1[i, pl.ds(8 * c, 8), :] = left[0] + left[1]
        both = T1[i, pl.ds(0, 8, stride=2), :] + T1[i, pl.ds(1, 8, stride=2), :]
        F2[4 * g + i, 8:16, :] = 0.125 * pair(both, 1)
    for copy in first2 + late1:
        copy.start()

    for copy in first2:
        copy.wait_recv()

    def start2(q):
        for c in range(3):
            rows = pl.ds(8 * c, 8)
            B2[q + 2, rows, :] = F2[q, rows, :] * INV2[q, rows, :] * (RF2[q // 2, rows, :] * RPS[2])

    def spread2(v_ref, q, row):
        rows = pl.ds(row, 8)
        x = q // 2
        centre = v_ref[q + 2, rows, :]
        total = (
            weighted(AXP2[x, rows, :] if q % 2 else None, v_ref[q + 3, rows, :])
            + weighted(None if q % 2 else AXM2[x, rows, :], v_ref[q + 1, rows, :])
            + AYP2[x, rows, :] * v_ref[q + 2, pl.ds(row + 1, 8), :]
            + AYM2[x, rows, :] * v_ref[q + 2, pl.ds(row - 1, 8), :]
            + BU[2] * zup(centre, 2)
            + BD[2] * zdn(centre, 2)
        )
        return centre, total

    def relax2(src, dst, fresh):
        for q in range(16):
            for c in range(2):
                rows = pl.ds(8 * c + 4, 8)
                centre, total = spread2(src, q, 8 * c + 4)
                kept = (1.0 + KEEP) * centre if fresh else KEEP * centre + B2[q + 2, rows, :]
                dst[q + 2, rows, :] = kept + INV2[q, rows, :] * total

    for q in range(16):
        start2(q)
    relax2(B2, V2, True)
    place = (sub >> 1) + lax.div(d, blocks)
    packed = zero
    for x in range(8):
        left = []
        for q in (2 * x, 2 * x + 1):
            centre, total = spread2(V2, q, 8)
            hp = HF2[x, 8:16, :] * permits[2]
            left.append(F2[q, 8:16, :] - hp * ((A2[q, 8:16, :] + BS[2]) * centre - total))
        both = pair(left[0] + left[1], 2)
        both = jnp.where(((place ^ lane) & 3) == 0, both, 0.0)
        packed = jnp.where(sub == x, jnp.sum(both, axis=0, keepdims=True), packed)
    G[pl.ds(d, 1), :, :] = (0.125 * packed)[None]

    def tell(k, carry):
        pltpu.make_async_remote_copy(
            src_ref=G.at[d],
            dst_ref=G.at[d],
            send_sem=s3_send,
            recv_sem=s3_recv,
            device_id=(g, lax.rem(d + k, devs)),
            device_id_type=MESH,
        ).start()
        return carry

    lax.fori_loop(1, devs, tell, 0)

    def wrap(k, ref):
        count = counts[k]
        ref[k, 0, :, :] = jnp.where((lane & 3) == 0, 0.0, roll(ref[k, count, :, :], 1))
        ref[k, count + 1, :, :] = jnp.where((lane & 3) == 3, 0.0, roll(ref[k, 1, :, :], -1))

    for e in range(counts[0]):
        FC[0, e + 1, :, :] = permute(fills, counts[0] * (lane & 3) + e)
    for e in range(counts[1]):
        FC[1, e + 1, :, :] = 0.25 * spair(FC[0, 2 * e + 1, :, :] + FC[0, 2 * e + 2, :, :], 1)
    for e in range(counts[2]):
        FC[2, e + 1, :, :] = 0.25 * spair(FC[1, 2 * e + 1, :, :] + FC[1, 2 * e + 2, :, :], 2)
    for k in range(3):
        wrap(k, FC)
        level = k + 3
        step = 1 << k
        last, first = sub >= 8 - step, sub < step
        for e in range(1, counts[k] + 1):
            f = FC[k, e, :, :]
            rf = 1.0 / f
            ayp = half(FC[k, e + 1, :, :] * rf)
            aym = half(FC[k, e - 1, :, :] * rf)
            axp = half(jnp.where(last, 0.0, sroll(f, -step) * rf))
            axm = half(jnp.where(first, 0.0, sroll(f, step) * rf))
            AYPC[k, e, :, :] = ayp
            AYMC[k, e, :, :] = aym
            if k == 2:
                AXPC[k, e, :, :] = jnp.where(last, axm, axp)
            else:
                AXPC[k, e, :, :] = jnp.where(last, 0.0, axp)
                AXMC[k, e, :, :] = jnp.where(first, 0.0, axm)
            a = ayp + aym + axp + axm
            AC[k, e, :, :] = a
            inv = OMEGA / (a + BS[level])
            INVC[k, e, :, :] = inv
            WC[k, e, :, :] = inv * rf * (4.0**level * RPS[level])

    for copy in late0:
        copy.wait_recv()
    for q in (0, 1, 22, 23):
        for c in range(5):
            start0(q, 8 * c - 4, 8)
    for q in (1, 2, 21, 22):
        for c in range(5):
            relax0(B0, V0, True, q, c)
    for copy in late1:
        copy.wait_recv()
    for q in (0, 1, 2, 15, 16, 17):
        start1(q)
    for q in (1, 2, 3, 14, 15, 16):
        relax1(B1, V1, True, q)

    pltpu.make_async_copy(G.at[0 : devs - 1], G.at[0 : devs - 1], s3_recv).wait()

    spot = lane & 3
    for m in range(blocks):
        parts = [G[b * blocks + m, :, :] for b in range(4)]
        for y in range(4):
            pick = [parts[(p - y) % 4] for p in range(4)]
            v = jnp.where(spot < 2, jnp.where(spot == 0, pick[0], pick[1]), jnp.where(spot == 2, pick[2], pick[3]))
            if y:
                v = jnp.where(spot + y < 4, roll(v, -y), roll(v, 4 - y))
            F3[4 * m + y, :, :] = v

    def spread_coarse(k, v_ref, e):
        level = k + 3
        step = 1 << k
        centre = v_ref[k, e, :, :]
        total = (
            AXPC[k, e, :, :] * sroll(centre, -step)
            + AXMC[k, e, :, :] * sroll(centre, step)
            + AYPC[k, e, :, :] * v_ref[k, e + 1, :, :]
            + AYMC[k, e, :, :] * v_ref[k, e - 1, :, :]
            + BU[level] * zup(centre, level)
            + BD[level] * zdn(centre, level)
        )
        return centre, total

    def start_coarse(k, f_ref):
        for e in range(1, counts[k] + 1):
            BC[k, e, :, :] = f_ref[e - 1, :, :] * WC[k, e, :, :]
        wrap(k, BC)

    def relax_coarse(k, src, dst, fresh=False):
        for e in range(1, counts[k] + 1):
            centre, total = spread_coarse(k, src, e)
            kept = (1.0 + KEEP) * centre if fresh else KEEP * centre + BC[k, e, :, :]
            dst[k, e, :, :] = kept + INVC[k, e, :, :] * total
        wrap(k, dst)

    def down_coarse(k, f_ref, next_ref):
        level = k + 3
        for e in range(counts[k + 1]):
            left = []
            for q in (2 * e + 1, 2 * e + 2):
                centre, total = spread_coarse(k, VC, q)
                hp = FC[k, q, :, :] * (0.25**level * permits[level])
                left.append(f_ref[q - 1, :, :] - hp * ((AC[k, q, :, :] + BS[level]) * centre - total))
            next_ref[e, :, :] = 0.125 * pair(spair(left[0] + left[1], 1 << k), 1 << (level - 1))

    for k, f_ref, next_ref in ((0, F3, F4), (1, F4, F5)):
        start_coarse(k, f_ref)
        relax_coarse(k, BC, VC, fresh=True)
        down_coarse(k, f_ref, next_ref)
    start_coarse(2, F5)

    def sweep(i, values):
        before = jnp.where(spot == 0, 0.0, roll(values[-1], 1))
        after = jnp.where(spot == 3, 0.0, roll(values[0], -1))
        padded = (before,) + tuple(values) + (after,)
        out = []
        for e in range(1, counts[2] + 1):
            centre = padded[e]
            total = (
                AXPC[2, e, :, :] * sroll(centre, 4)
                + AYPC[2, e, :, :] * padded[e + 1]
                + AYMC[2, e, :, :] * padded[e - 1]
                + BU[5] * zup(centre, 5)
                + BD[5] * zdn(centre, 5)
            )
            out.append(KEEP * centre + BC[2, e, :, :] + INVC[2, e, :, :] * total)
        return tuple(out)

    values = tuple(BC[2, e, :, :] for e in range(1, counts[2] + 1))
    values = lax.fori_loop(0, SWEEPS - 1, sweep, values)
    for e in range(1, counts[2] + 1):
        VC[2, e, :, :] = values[e - 1]
    for k in (1, 0):
        for e in range(counts[k]):
            VC[k, e + 1, :, :] = VC[k, e + 1, :, :] + VC[k + 1, e // 2 + 1, :, :]
        wrap(k, VC)
        relax_coarse(k, VC, WC)
        relax_coarse(k, WC, VC)

    for j in range(8):
        y = 4 * d + j - 2
        inside = (y >= 0) & (y < 4 * devs)
        y = jnp.minimum(jnp.maximum(y, 0), 4 * devs - 1)
        tile = VC[0, lax.rem(y, counts[0]) + 1, :, :]
        mine = jnp.where(inside, lax.div(y, counts[0]), 4)
        UU[j, :, :] = pair(pair(jnp.where(spot == mine, tile, 0.0), 1), 2)
    for x in range(8):
        for c in range(2):
            rows = [jnp.broadcast_to(UU[4 * c + k, x : x + 1, :], (8, 128)) for k in range(4)]
            fine = jnp.where(
                sub < 4, jnp.where(sub < 2, rows[0], rows[1]), jnp.where(sub < 6, rows[2], rows[3])
            )
            at = pl.ds(8 * c + 4, 8)
            for q in (2 * x + 2, 2 * x + 3):
                V2[q, at, :] = V2[q, at, :] + fine
    relax2(V2, W2, False)
    relax2(W2, V2, False)

    for i in range(8):
        for row, count in ((6, 8), (14, 4)):
            fine = V2[4 * g + i, pl.ds(row, count), :]
            for odd in range(2):
                P1[i, pl.ds(2 * (row - 6) + odd, count, stride=2), :] = fine
        for q in (2 * i + 1, 2 * i + 2):
            for c in range(3):
                rows = pl.ds(8 * c + 4, 8)
                V1[q, rows, :] = V1[q, rows, :] + P1[i, 8 * c : 8 * c + 8, :]
    for q in range(2, 16):
        relax1(V1, W1, False, q)
    for q in range(3, 15):
        relax1(W1, V1, False, q)

    for i in range(12):
        for row, count in ((6, 8), (14, 8), (22, 4)):
            coarse = V1[i + 3, pl.ds(row, 8), :]
            fine = (permute(coarse, low_z), permute(coarse, high_z))
            for h in range(2):
                for odd in range(2):
                    P0[h, i, pl.ds(2 * (row - 6) + odd, count, stride=2), :] = fine[h][0:count, :]
        for q in (2 * i, 2 * i + 1):
            if not 1 <= q <= 22:
                continue
            for h in range(2):
                for c in range(5):
                    rows = pl.ds(8 * c + 8, 8)
                    V0[h, q, rows, :] = V0[h, q, rows, :] + P0[h, i, 8 * c : 8 * c + 8, :]
    for q in range(2, 22):
        for c in range(5):
            relax0(V0, W0, False, q, c)
    for q in range(3, 21):
        for c in range(5):
            relax0(W0, V0, False, q, c)

    for x in range(16):
        for c in range(4):
            centre, left = left0(V0, x + 4, c)
            for h in range(2):
                pot_ref[x, 8 * c : 8 * c + 8, h * 128 : h * 128 + 128] = centre[h]
                res_ref[x, 8 * c : 8 * c + 8, h * 128 : h * 128 + 128] = left[h]

    for copy in first0 + late0 + first1 + late1 + first2:
        copy.wait_send()
    pltpu.make_async_copy(G.at[0 : devs - 1], G.at[0 : devs - 1], s3_send).wait()


def solution(mesh):
    groups, devs = mesh.shape["group"], mesh.shape["dev"]

    def rows(*shape):
        return pltpu.VMEM(shape + (128,), jnp.float32)

    def sems(count):
        return pltpu.SemaphoreType.DMA((count,))

    def on_device(source, plane_layer, layer_permittivity, tile_kind, kind_fill):
        vmem = pl.BlockSpec(memory_space=pltpu.VMEM)
        hbm = pl.BlockSpec(memory_space=pl.ANY)
        tiles = devs + 2
        coarse = rows(3, tiles, 8)
        out = jax.ShapeDtypeStruct(source.shape, jnp.float32)
        scratch = [
            pltpu.VMEM((2, 128), jnp.int32), pltpu.VMEM(tile_kind.shape, jnp.int32),
            pltpu.SMEM(layer_permittivity.shape, jnp.float32), pltpu.SMEM(kind_fill.shape, jnp.float32),
            rows(2, 24, 48), rows(2, 24, 56), rows(2, 24, 56), rows(2, 24, 56),
            rows(2, 12, 40), rows(12, 40), rows(4, 40), rows(4, 40),
            rows(4, 40), rows(4, 40), rows(4, 40), rows(4, 40), rows(6, 64),
            rows(8, 2, 32), rows(2, 12, 40),
            rows(18, 32), rows(18, 32), rows(18, 32), rows(18, 32),
            rows(18, 32), rows(18, 32), rows(6, 32), rows(6, 32),
            rows(6, 32), rows(6, 32), rows(6, 32), rows(6, 32), rows(6, 48),
            rows(4, 16), rows(8, 24),
            rows(16, 24), rows(20, 24), rows(20, 24), rows(20, 24),
            rows(16, 24), rows(16, 24), rows(8, 24), rows(8, 24),
            rows(8, 24), rows(8, 24), rows(8, 24), rows(8, 24), rows(10, 40),
            rows(8, 8),
            rows(12, 24), rows(devs, 8), rows(devs, 8), rows(devs // 2, 8), rows(devs // 4, 8),
            coarse, coarse, coarse, coarse, coarse, coarse, coarse, coarse, coarse, coarse,
            sems(4), sems(2), sems(18), sems(18), sems(18), sems(18), sems(9), sems(9), sems(9), sems(9),
            sems(3 * groups - 1), sems(3 * groups - 1),
            pltpu.SemaphoreType.DMA, pltpu.SemaphoreType.DMA,
        ]
        return pl.pallas_call(
            functools.partial(kernel, groups, devs),
            out_shape=(out, out),
            in_specs=[hbm] * 5,
            out_specs=(vmem, vmem),
            scratch_shapes=scratch,
            compiler_params=pltpu.CompilerParams(
                collective_id=0, has_side_effects=True, vmem_limit_bytes=60 * 1024 * 1024
            ),
        )(plane_layer.reshape(2, 128), tile_kind, layer_permittivity, kind_fill, source)

    in_specs = (P("group", "dev", None), P(), P(), P(), P())
    out_specs = (P("group", "dev", None), P("group", "dev", None))
    return jax.shard_map(
        on_device, mesh=mesh, in_specs=in_specs, out_specs=out_specs, check_vma=False
    )
```

```python
import functools

import jax
import jax.numpy as jnp
from jax import lax
from jax.experimental import pallas as pl
from jax.experimental.pallas import tpu as pltpu
from jax.sharding import PartitionSpec as P

MESH = pl.DeviceIdType.MESH
OMEGA = 2.0 / 3.0
KEEP = 1.0 - OMEGA
SWEEPS = 24
NEIGHBOURS = ((-1, -1), (1, 1), (-1, 1), (1, -1), (-1, 0), (1, 0), (0, -1), (0, 1))


def kernel(
    groups,
    devs,
    layers_hbm,
    kinds_hbm,
    permit_hbm,
    fill_hbm,
    source,
    pot_ref,
    res_ref,
    layers_ref, kinds_ref, permit_ref, fill_ref,
    F0, V0, W0, B0, INV0, A0, AXP0, AXM0, AYP0, AYM0, RF0, HF0, FX0, T0, P0,
    F1, V1, W1, B1, INV1, A1, AXP1, AXM1, AYP1, AYM1, RF1, HF1, FX1, T1, P1,
    F2, F2P, V2, W2, B2, INV2, A2, AXP2, AXM2, AYP2, AYM2, RF2, HF2, FX2, UU,
    FA, G, F3, F4, F5, FC, VC, WC, BC, INVC, AC, AXPC, AXMC, AYPC, AYMC,
    input_sem, local_sem, s0_send, s0_recv, s0l_send, s0l_recv, s1_send, s1_recv, s1l_send, s1l_recv,
    s2_send, s2_recv, s3_send, s3_recv,
):
    g = lax.axis_index("group")
    d = lax.axis_index("dev")
    f32 = jnp.float32
    lane = lax.broadcasted_iota(jnp.int32, (8, 128), 1)
    sub = lax.broadcasted_iota(jnp.int32, (8, 128), 0)
    even = (lane & 1) == 0
    zero = jnp.zeros((8, 128), f32)
    blocks = devs // 4
    counts = (4 * blocks, 2 * blocks, blocks)

    def peer(dx, dy):
        return (lax.rem(g + dx + groups, groups), lax.rem(d + dy + devs, devs))

    def roll(v, shift):
        return pltpu.roll(v, shift % 128, 1)

    def sroll(v, shift):
        return pltpu.roll(v, shift % 8, 0)

    def permute(v, index):
        return jnp.take_along_axis(v, index, axis=1, mode="promise_in_bounds")

    barrier = pltpu.get_barrier_semaphore()
    column = [(dx, dy) for dx in range(groups) for dy in (-1, 0, 1) if (dx, dy) != (0, 0)]
    for dx, dy in column:
        pl.semaphore_signal(barrier, inc=1, device_id=peer(dx, dy), device_id_type=MESH)

    def greet(k, carry):
        pl.semaphore_signal(barrier, inc=1, device_id=(g, lax.rem(d + k, devs)), device_id_type=MESH)
        return carry

    inputs = [
        pltpu.make_async_copy(src, dst, input_sem.at[i])
        for i, (src, dst) in enumerate(
            (
                (layers_hbm, layers_ref),
                (kinds_hbm, kinds_ref),
                (permit_hbm, permit_ref),
                (fill_hbm, fill_ref),
            )
        )
    ]
    own = [
        pltpu.make_async_copy(
            source.at[:, :, h * 128 : h * 128 + 128], F0.at[h, 4:20, 8:40, :], local_sem.at[h]
        )
        for h in range(2)
    ]
    for copy in inputs:
        copy.start()
    lax.fori_loop(2, devs - 1, greet, 0)
    for copy in own:
        copy.start()

    def halo0(dx, dy, h, late):
        px = {0: (0, 16, 4), 1: (14, 2, 2), -1: (0, 2, 20)}[dx]
        if late:
            px = {1: (12, 2, 0), -1: (2, 2, 22)}[dx]
        py = {0: (0, 32, 8), 1: (24, 8, 0), -1: (0, 8, 40)}[dy]
        slot = ((dx + 1) * 3 + dy + 1) * 2 + h
        send, recv = (s0l_send, s0l_recv) if late else (s0_send, s0_recv)
        return pltpu.make_async_remote_copy(
            src_ref=source.at[px[0] : px[0] + px[1], py[0] : py[0] + py[1], h * 128 : h * 128 + 128],
            dst_ref=F0.at[h, px[2] : px[2] + px[1], py[2] : py[2] + py[1], :],
            send_sem=send.at[slot],
            recv_sem=recv.at[slot],
            device_id=peer(dx, dy),
            device_id_type=MESH,
        )

    first0 = [halo0(dx, dy, h, False) for dx, dy in NEIGHBOURS for h in range(2)]
    late0 = [halo0(dx, dy, h, True) for dx, dy in NEIGHBOURS if dx for h in range(2)]

    def halo1(dx, dy, late):
        px = {0: (0, 8, 5), 1: (6, 2, 3), -1: (0, 2, 13)}[dx]
        if late:
            px = {1: (3, 3, 0), -1: (2, 3, 15)}[dx]
        py = {0: (0, 16, 8), 1: (8, 8, 0), -1: (0, 8, 24)}[dy]
        slot = (dx + 1) * 3 + dy + 1
        send, recv = (s1l_send, s1l_recv) if late else (s1_send, s1_recv)
        return pltpu.make_async_remote_copy(
            src_ref=F1.at[px[0] + 5 : px[0] + px[1] + 5, py[0] + 8 : py[0] + py[1] + 8, :],
            dst_ref=F1.at[px[2] : px[2] + px[1], py[2] : py[2] + py[1], :],
            send_sem=send.at[slot],
            recv_sem=recv.at[slot],
            device_id=peer(dx, dy),
            device_id_type=MESH,
        )

    first1 = [halo1(dx, dy, False) for dx, dy in NEIGHBOURS]
    late1 = [halo1(dx, dy, True) for dx, dy in NEIGHBOURS if dx]

    def block2(slot):
        dx, dy = column[slot]
        return pltpu.make_async_remote_copy(
            src_ref=F2P.at[pl.ds(2 * g, 2), 8:16, :],
            dst_ref=F2P.at[pl.ds(2 * g, 2), 8 - 8 * dy : 16 - 8 * dy, :],
            send_sem=s2_send.at[slot],
            recv_sem=s2_recv.at[slot],
            device_id=peer(dx, dy),
            device_id_type=MESH,
        )

    first2 = [block2(slot) for slot in range(len(column))]

    for copy in inputs:
        copy.wait()
    kinds = kinds_ref[...]
    fills = zero
    for kind in range(fill_ref.shape[0]):
        fills = jnp.where(kinds == kind, fill_ref[kind], fills)
    fills = jnp.where(lane < 4 * devs, fills, 0.0)
    shifted = pltpu.roll(fills, lax.rem(8 + 128 - 4 * d + 128, 128), 1)
    tile_y = 4 * d - 8 + lane
    shifted = jnp.where((tile_y >= 0) & (tile_y < 4 * devs), shifted, 0.0)
    for c in range(3):
        for x in (0, 1, 10, 11):
            FA[x, 8 * c : 8 * c + 8, :] = zero
        for x in range(8):
            row = jnp.broadcast_to(shifted[x : x + 1, :], (8, 128))
            picked = jnp.sum(jnp.where(lane == sub + 8 * c, row, 0.0), axis=1, keepdims=True)
            FA[x + 2, 8 * c : 8 * c + 8, :] = jnp.broadcast_to(picked, (8, 128))

    permit0 = []
    for h in range(2):
        layer = jnp.broadcast_to(layers_ref[h : h + 1, :], (8, 128))
        value = zero
        for k in range(permit_ref.shape[0]):
            value = jnp.where(layer == k, permit_ref[k], value)
        permit0.append(value)

    def zup0(h0, h1):
        r0, r1 = roll(h0, -1), roll(h1, -1)
        return jnp.where(lane == 127, r1, r0), r1

    def zdn0(h0, h1):
        r0, r1 = roll(h0, 1), roll(h1, 1)
        return r0, jnp.where(lane == 0, r0, r1)

    def zup(v, level):
        return roll(v, -(1 << (level - 1)))

    def zdn(v, level):
        return roll(v, 1 << (level - 1))

    def pair(v, step):
        return v + jnp.where((lane & step) == 0, roll(v, -step), roll(v, step))

    def spair(v, step):
        return v + jnp.where((sub & step) == 0, sroll(v, -step), sroll(v, step))

    gather_z = jnp.where(lane < 64, 2 * lane, 2 * lane - 127)
    low_z = lane >> 1
    high_z = low_z + 64

    def halves(h0, h1):
        both = jnp.where(even, h0, h1) + jnp.where(even, roll(h0, -1), roll(h1, 1))
        return permute(both, gather_z)

    pu0, pu1 = zup0(*permit0)
    pd0, pd1 = zdn0(*permit0)
    RP0 = [1.0 / p for p in permit0]
    ru = [pu0 * RP0[0], jnp.where(lane == 127, 0.0, pu1 * RP0[1])]
    rd = [jnp.where(lane == 0, 0.0, pd0 * RP0[0]), pd1 * RP0[1]]
    BU0 = [0.5 + 0.5 * ru[0], jnp.where(lane == 127, 0.0, 0.5 + 0.5 * ru[1])]
    BD0 = [jnp.where(lane == 0, 0.0, 0.5 + 0.5 * rd[0]), 0.5 + 0.5 * rd[1]]
    BS0 = [1.0 + 0.5 * (ru[h] + rd[h]) for h in range(2)]
    permits = [None, 0.5 * halves(*permit0)]
    for level in (2, 3, 4, 5):
        permits.append(0.5 * pair(permits[level - 1], 1 << (level - 2)))
    RPS, BU, BD, BS = [None], [None], [None], [None]
    for level in range(1, 6):
        p = permits[level]
        step = 1 << (level - 1)
        rp = 1.0 / p
        top, bottom = lane >= 128 - step, lane < step
        up = jnp.where(top, 0.0, zup(p, level) * rp)
        dn = jnp.where(bottom, 0.0, zdn(p, level) * rp)
        RPS.append(rp)
        BU.append(jnp.where(top, 0.0, 0.5 + 0.5 * up))
        BD.append(jnp.where(bottom, 0.0, 0.5 + 0.5 * dn))
        BS.append(1.0 + 0.5 * (up + dn))

    for t in range(6):
        for j in range(8):
            FX0[t, 8 * j : 8 * j + 8, :] = jnp.broadcast_to(FA[2 * g + t, 6 + j : 7 + j, :], (8, 128))

    def half(ratio):
        return 0.5 + 0.5 * ratio

    for c in range(5):
        at = 8 * c
        out = pl.ds(at, 8)
        for t in range(4):
            f = FX0[t + 1, pl.ds(at + 12, 8), :]
            inside = f > 0.0
            rf = 1.0 / jnp.where(inside, f, 1.0)
            ayp = half(FX0[t + 1, pl.ds(at + 13, 8), :] * rf)
            aym = half(FX0[t + 1, pl.ds(at + 11, 8), :] * rf)
            axp = half(FX0[t + 2, pl.ds(at + 12, 8), :] * rf)
            axm = half(FX0[t, pl.ds(at + 12, 8), :] * rf)
            AYP0[t, out, :] = ayp
            AYM0[t, out, :] = aym
            AXP0[t, out, :] = axp
            AXM0[t, out, :] = axm
            RF0[t, out, :] = rf
            HF0[t, out, :] = f
            for kind in range(3):
                if (t, kind) in ((0, 0), (3, 2)):
                    continue
                a = ayp + aym + (axp if kind == 2 else 1.0) + (axm if kind == 0 else 1.0)
                A0[3 * t + kind, out, :] = a
                for h in range(2):
                    INV0[h, 3 * t + kind, out, :] = jnp.where(inside, OMEGA / (a + BS0[h]), 0.0)

    pl.semaphore_wait(barrier, len(column) + devs - 3)
    for copy in first0 + late0:
        copy.start()

    for t in range(6):
        for j in range(6):
            FX1[t, 8 * j : 8 * j + 8, :] = jnp.where(
                sub < 4,
                jnp.broadcast_to(FA[2 * g + t, 4 + 2 * j : 5 + 2 * j, :], (8, 128)),
                jnp.broadcast_to(FA[2 * g + t, 5 + 2 * j : 6 + 2 * j, :], (8, 128)),
            )

    def weights1(c, carry):
        at = pl.multiple_of(8 * c, 8)
        out = pl.ds(at, 8)
        for t in range(6):
            f = FX1[t, pl.ds(at + 8, 8), :]
            inside = f > 0.0
            rf = 1.0 / jnp.where(inside, f, 1.0)
            ayp = half(FX1[t, pl.ds(at + 9, 8), :] * rf)
            aym = half(FX1[t, pl.ds(at + 7, 8), :] * rf)
            AYP1[t, out, :] = ayp
            AYM1[t, out, :] = aym
            RF1[t, out, :] = 4.0 * rf
            HF1[t, out, :] = 0.25 * f
            ay = ayp + aym
            axp = half(FX1[t + 1, pl.ds(at + 8, 8), :] * rf) if t < 5 else None
            axm = half(FX1[t - 1, pl.ds(at + 8, 8), :] * rf) if t > 0 else None
            if t < 5:
                AXP1[t, out, :] = axp
            if t > 0:
                AXM1[t, out, :] = axm
            for r in range(4):
                q = 4 * t + r - 3
                if q < 0 or q > 17 or r == 2:
                    continue
                a = ay + (axp if r == 3 else 1.0) + (axm if r == 0 else 1.0)
                A1[3 * t + min(r, 2), out, :] = a
                INV1[3 * t + min(r, 2), out, :] = jnp.where(inside, OMEGA / (a + BS[1]), 0.0)
        return carry

    lax.fori_loop(0, 4, weights1, 0)

    for x in range(10):
        for j in range(5):
            rows = [jnp.broadcast_to(FA[x + 1, 4 * j + k : 4 * j + k + 1, :], (8, 128)) for k in range(4)]
            FX2[x, 8 * j : 8 * j + 8, :] = jnp.where(
                sub < 4, jnp.where(sub < 2, rows[0], rows[1]), jnp.where(sub < 6, rows[2], rows[3])
            )

    def weights2(x, carry):
        for c in range(3):
            out = pl.ds(8 * c, 8)
            f = FX2[x + 1, 8 * c + 8 : 8 * c + 16, :]
            inside = f > 0.0
            rf = 1.0 / jnp.where(inside, f, 1.0)
            ayp = half(FX2[x + 1, pl.ds(8 * c + 9, 8), :] * rf)
            aym = half(FX2[x + 1, pl.ds(8 * c + 7, 8), :] * rf)
            axp = half(FX2[x + 2, 8 * c + 8 : 8 * c + 16, :] * rf)
            axm = half(FX2[x, 8 * c + 8 : 8 * c + 16, :] * rf)
            AYP2[x, out, :] = ayp
            AYM2[x, out, :] = aym
            AXP2[x, out, :] = axp
            AXM2[x, out, :] = axm
            RF2[x, out, :] = 16.0 * rf
            HF2[x, out, :] = 0.0625 * f
            for r in range(2):
                a = ayp + aym + (axp if r == 1 else axm) + 1.0
                A2[2 * x + r, out, :] = a
                INV2[2 * x + r, out, :] = jnp.where(inside, OMEGA / (a + BS[2]), 0.0)
        return carry

    lax.fori_loop(0, 8, weights2, 0)
    for ref in (B2, V2, W2):
        for x in (0, 1, 18, 19):
            for c in range(3):
                ref[x, 8 * c : 8 * c + 8, :] = zero

    def kind0(q):
        t, r = (q + 4) // 8, (q + 4) % 8
        kind = 0 if r == 0 else 2 if r == 7 else 1
        return t, kind, 3 * t + kind

    def start0(q, y, count):
        t, _, cls = kind0(q)
        w = pl.ds(y + 4, count)
        rf = RF0[t, w, :]
        for h in range(2):
            f = F0[h, q, pl.ds(y + 8, count), :]
            B0[h, q, pl.ds(y + 12, count), :] = f * INV0[h, cls, w, :] * (rf * RP0[h][0:count, :])

    def weighted(weight, v):
        return v if weight is None else weight * v

    def spread0(v_ref, q, y):
        t, kind, _ = kind0(q)
        w = pl.ds(y + 4, 8)
        axp = AXP0[t, w, :] if kind == 2 else None
        axm = AXM0[t, w, :] if kind == 0 else None
        ayp, aym = AYP0[t, w, :], AYM0[t, w, :]
        centre = [v_ref[h, q, pl.ds(y + 12, 8), :] for h in range(2)]
        up, dn = zup0(*centre), zdn0(*centre)
        total = []
        for h in range(2):
            total.append(
                weighted(axp, v_ref[h, q + 1, pl.ds(y + 12, 8), :])
                + weighted(axm, v_ref[h, q - 1, pl.ds(y + 12, 8), :])
                + ayp * v_ref[h, q, pl.ds(y + 13, 8), :]
                + aym * v_ref[h, q, pl.ds(y + 11, 8), :]
                + BU0[h] * up[h]
                + BD0[h] * dn[h]
            )
        return centre, total

    def relax0(src, dst, fresh, q, c):
        cls = kind0(q)[2]
        y = 8 * c - 4
        centre, total = spread0(src, q, y)
        for h in range(2):
            if fresh:
                kept = (1.0 + KEEP) * centre[h]
            else:
                kept = KEEP * centre[h] + B0[h, q, pl.ds(y + 12, 8), :]
            dst[h, q, pl.ds(y + 12, 8), :] = kept + INV0[h, cls, pl.ds(y + 4, 8), :] * total[h]

    def left0(v_ref, q, c):
        t, _, cls = kind0(q)
        centre, total = spread0(v_ref, q, 8 * c)
        a = A0[cls, pl.ds(8 * c + 4, 8), :]
        hf = HF0[t, pl.ds(8 * c + 4, 8), :]
        left = []
        for h in range(2):
            f = F0[h, q, pl.ds(8 * c + 8, 8), :]
            left.append(f - hf * permit0[h] * ((a + BS0[h]) * centre[h] - total[h]))
        return centre, left

    for copy in own:
        copy.wait()
    for q in range(4, 20):
        for c in range(4):
            start0(q, 8 * c, 8)
    for q in range(5, 19):
        for c in range(1, 4):
            relax0(B0, V0, True, q, c)
    def down0(i, c):
        first = left0(V0, 2 * i + 4, c)[1]
        second = left0(V0, 2 * i + 5, c)[1]
        for h in range(2):
            T0[i, h, pl.ds(8 * c, 8), :] = first[h] + second[h]

    for i in range(1, 7):
        for c in (1, 2):
            down0(i, c)
    for copy in first0:
        copy.wait_recv()
    for q in range(2, 22):
        if 4 <= q < 20:
            start0(q, -4, 4)
            start0(q, 32, 4)
        else:
            for c in range(5):
                start0(q, 8 * c - 4, 8)
    for q in range(3, 21):
        for c in (0, 4) if 5 <= q < 19 else range(5):
            relax0(B0, V0, True, q, c)

    for i in range(8):
        for c in (0, 3) if 1 <= i < 7 else range(4):
            down0(i, c)
        for c in range(2):
            both = [
                T0[i, h, pl.ds(16 * c, 8, stride=2), :] + T0[i, h, pl.ds(16 * c + 1, 8, stride=2), :]
                for h in range(2)
            ]
            F1[i + 5, 8 * c + 8 : 8 * c + 16, :] = 0.125 * halves(*both)
    for copy in first1:
        copy.start()

    for copy in first1:
        copy.wait_recv()

    def kind1(q):
        t, r = (q + 3) // 4, (q + 3) % 4
        return t, r, 3 * t + (0, 1, 1, 2)[r]

    def start1(q):
        t, _, cls = kind1(q)
        for c in range(4):
            rows = pl.ds(8 * c, 8)
            B1[q, rows, :] = F1[q, rows, :] * INV1[cls, rows, :] * (RF1[t, rows, :] * RPS[1])

    def spread1(v_ref, q, row):
        t, r, _ = kind1(q)
        rows = pl.ds(row, 8)
        axp = AXP1[t, rows, :] if r == 3 else None
        axm = AXM1[t, rows, :] if r == 0 else None
        centre = v_ref[q, rows, :]
        total = (
            weighted(axp, v_ref[q + 1, rows, :])
            + weighted(axm, v_ref[q - 1, rows, :])
            + AYP1[t, rows, :] * v_ref[q, pl.ds(row + 1, 8), :]
            + AYM1[t, rows, :] * v_ref[q, pl.ds(row - 1, 8), :]
            + BU[1] * zup(centre, 1)
            + BD[1] * zdn(centre, 1)
        )
        return centre, total

    def relax1(src, dst, fresh, q):
        cls = kind1(q)[2]
        for c in range(3):
            rows = pl.ds(8 * c + 4, 8)
            centre, total = spread1(src, q, 8 * c + 4)
            kept = (1.0 + KEEP) * centre if fresh else KEEP * centre + B1[q, rows, :]
            dst[q, rows, :] = kept + INV1[cls, rows, :] * total

    for q in range(3, 15):
        start1(q)
    for q in range(4, 14):
        relax1(B1, V1, True, q)
    sent = []
    for i in range(4):
        for c in range(2):
            rows = pl.ds(8 * c + 8, 8)
            left = []
            for q in (2 * i + 5, 2 * i + 6):
                t, _, cls = kind1(q)
                centre, total = spread1(V1, q, 8 * c + 8)
                hp = HF1[t, rows, :] * permits[1]
                left.append(F1[q, rows, :] - hp * ((A1[cls, rows, :] + BS[1]) * centre - total))
            T1[i, pl.ds(8 * c, 8), :] = left[0] + left[1]
        both = T1[i, pl.ds(0, 8, stride=2), :] + T1[i, pl.ds(1, 8, stride=2), :]
        sent.append(0.125 * pair(both, 1))
    for i in range(2):
        F2P[2 * g + i, 8:16, :] = jnp.where(even, sent[2 * i], sent[2 * i + 1])
    for copy in first2 + late1:
        copy.start()

    for copy in first2:
        copy.wait_recv()

    def start2(x):
        for c in range(3):
            rows = pl.ds(8 * c, 8)
            both = F2P[x, rows, :]
            scale = RF2[x, rows, :] * RPS[2]
            planes = (jnp.where(even, both, roll(both, 1)), jnp.where(even, roll(both, -1), both))
            for q in (2 * x, 2 * x + 1):
                if c == 1:
                    F2[q, rows, :] = planes[q % 2]
                B2[q + 2, rows, :] = planes[q % 2] * INV2[q, rows, :] * scale

    def spread2(v_ref, q, row):
        rows = pl.ds(row, 8)
        x = q // 2
        centre = v_ref[q + 2, rows, :]
        total = (
            weighted(AXP2[x, rows, :] if q % 2 else None, v_ref[q + 3, rows, :])
            + weighted(None if q % 2 else AXM2[x, rows, :], v_ref[q + 1, rows, :])
            + AYP2[x, rows, :] * v_ref[q + 2, pl.ds(row + 1, 8), :]
            + AYM2[x, rows, :] * v_ref[q + 2, pl.ds(row - 1, 8), :]
            + BU[2] * zup(centre, 2)
            + BD[2] * zdn(centre, 2)
        )
        return centre, total

    def relax2(src, dst, fresh):
        for q in range(16):
            for c in range(2):
                rows = pl.ds(8 * c + 4, 8)
                centre, total = spread2(src, q, 8 * c + 4)
                kept = (1.0 + KEEP) * centre if fresh else KEEP * centre + B2[q + 2, rows, :]
                dst[q + 2, rows, :] = kept + INV2[q, rows, :] * total

    for x in range(8):
        start2(x)
    relax2(B2, V2, True)
    place = (sub >> 1) + lax.div(d, blocks)
    packed = zero
    for x in range(8):
        left = []
        for q in (2 * x, 2 * x + 1):
            centre, total = spread2(V2, q, 8)
            hp = HF2[x, 8:16, :] * permits[2]
            left.append(F2[q, 8:16, :] - hp * ((A2[q, 8:16, :] + BS[2]) * centre - total))
        both = pair(left[0] + left[1], 2)
        both = jnp.where(((place ^ lane) & 3) == 0, both, 0.0)
        packed = jnp.where(sub == x, jnp.sum(both, axis=0, keepdims=True), packed)
    G[pl.ds(d, 1), :, :] = (0.125 * packed)[None]

    square = next((n for n in range(2, devs) if 2 * n * n == devs), 0)

    def hops(k):
        if not square:
            return k
        apart = (k // 2 % square, k // (2 * square))
        return sum(min(n, square - n) for n in apart) + 0.5 * (k % 2)

    for k in sorted(range(1, devs), key=hops, reverse=True):
        if square:
            y = lax.rem(lax.div(d, 2 * square) + k // (2 * square), square)
            z = lax.rem(lax.rem(lax.div(d, 2), square) + k // 2 % square, square)
            to = 2 * (square * y + z) + lax.rem(lax.rem(d, 2) + k % 2, 2)
        else:
            to = lax.rem(d + k, devs)
        pltpu.make_async_remote_copy(
            src_ref=G.at[d],
            dst_ref=G.at[d],
            send_sem=s3_send,
            recv_sem=s3_recv,
            device_id=(g, to),
            device_id_type=MESH,
        ).start()

    def wrap(k, ref):
        count = counts[k]
        ref[k, 0, :, :] = jnp.where((lane & 3) == 0, 0.0, roll(ref[k, count, :, :], 1))
        ref[k, count + 1, :, :] = jnp.where((lane & 3) == 3, 0.0, roll(ref[k, 1, :, :], -1))

    for e in range(counts[0]):
        FC[0, e + 1, :, :] = permute(fills, counts[0] * (lane & 3) + e)
    for e in range(counts[1]):
        FC[1, e + 1, :, :] = 0.25 * spair(FC[0, 2 * e + 1, :, :] + FC[0, 2 * e + 2, :, :], 1)
    for e in range(counts[2]):
        FC[2, e + 1, :, :] = 0.25 * spair(FC[1, 2 * e + 1, :, :] + FC[1, 2 * e + 2, :, :], 2)
    for k in range(3):
        wrap(k, FC)
        level = k + 3
        step = 1 << k
        last, first = sub >= 8 - step, sub < step
        for e in range(1, counts[k] + 1):
            f = FC[k, e, :, :]
            rf = 1.0 / f
            ayp = half(FC[k, e + 1, :, :] * rf)
            aym = half(FC[k, e - 1, :, :] * rf)
            axp = half(jnp.where(last, 0.0, sroll(f, -step) * rf))
            axm = half(jnp.where(first, 0.0, sroll(f, step) * rf))
            AYPC[k, e, :, :] = ayp
            AYMC[k, e, :, :] = aym
            if k == 2:
                AXPC[k, e, :, :] = jnp.where(last, axm, axp)
            else:
                AXPC[k, e, :, :] = jnp.where(last, 0.0, axp)
                AXMC[k, e, :, :] = jnp.where(first, 0.0, axm)
            a = ayp + aym + axp + axm
            AC[k, e, :, :] = a
            inv = OMEGA / (a + BS[level])
            INVC[k, e, :, :] = inv
            WC[k, e, :, :] = inv * rf * (4.0**level * RPS[level])

    for copy in late0:
        copy.wait_recv()
    for q in (0, 1, 22, 23):
        for c in range(5):
            start0(q, 8 * c - 4, 8)
    for q in (1, 2, 21, 22):
        for c in range(5):
            relax0(B0, V0, True, q, c)
    for copy in late1:
        copy.wait_recv()
    for q in (0, 1, 2, 15, 16, 17):
        start1(q)
    for q in (1, 2, 3, 14, 15, 16):
        relax1(B1, V1, True, q)

    pltpu.make_async_copy(G.at[0 : devs - 1], G.at[0 : devs - 1], s3_recv).wait()

    spot = lane & 3
    for m in range(blocks):
        parts = [G[b * blocks + m, :, :] for b in range(4)]
        for y in range(4):
            pick = [parts[(p - y) % 4] for p in range(4)]
            v = jnp.where(spot < 2, jnp.where(spot == 0, pick[0], pick[1]), jnp.where(spot == 2, pick[2], pick[3]))
            if y:
                v = jnp.where(spot + y < 4, roll(v, -y), roll(v, 4 - y))
            F3[4 * m + y, :, :] = v

    def spread_coarse(k, v_ref, e):
        level = k + 3
        step = 1 << k
        centre = v_ref[k, e, :, :]
        total = (
            AXPC[k, e, :, :] * sroll(centre, -step)
            + AXMC[k, e, :, :] * sroll(centre, step)
            + AYPC[k, e, :, :] * v_ref[k, e + 1, :, :]
            + AYMC[k, e, :, :] * v_ref[k, e - 1, :, :]
            + BU[level] * zup(centre, level)
            + BD[level] * zdn(centre, level)
        )
        return centre, total

    def start_coarse(k, f_ref):
        for e in range(1, counts[k] + 1):
            BC[k, e, :, :] = f_ref[e - 1, :, :] * WC[k, e, :, :]
        wrap(k, BC)

    def relax_coarse(k, src, dst, fresh=False):
        for e in range(1, counts[k] + 1):
            centre, total = spread_coarse(k, src, e)
            kept = (1.0 + KEEP) * centre if fresh else KEEP * centre + BC[k, e, :, :]
            dst[k, e, :, :] = kept + INVC[k, e, :, :] * total
        wrap(k, dst)

    def down_coarse(k, f_ref, next_ref):
        level = k + 3
        for e in range(counts[k + 1]):
            left = []
            for q in (2 * e + 1, 2 * e + 2):
                centre, total = spread_coarse(k, VC, q)
                hp = FC[k, q, :, :] * (0.25**level * permits[level])
                left.append(f_ref[q - 1, :, :] - hp * ((AC[k, q, :, :] + BS[level]) * centre - total))
            next_ref[e, :, :] = 0.125 * pair(spair(left[0] + left[1], 1 << k), 1 << (level - 1))

    for k, f_ref, next_ref in ((0, F3, F4), (1, F4, F5)):
        start_coarse(k, f_ref)
        relax_coarse(k, BC, VC, fresh=True)
        down_coarse(k, f_ref, next_ref)
    start_coarse(2, F5)

    def sweep(i, values):
        before = jnp.where(spot == 0, 0.0, roll(values[-1], 1))
        after = jnp.where(spot == 3, 0.0, roll(values[0], -1))
        padded = (before,) + tuple(values) + (after,)
        out = []
        for e in range(1, counts[2] + 1):
            centre = padded[e]
            total = (
                AXPC[2, e, :, :] * sroll(centre, 4)
                + AYPC[2, e, :, :] * padded[e + 1]
                + AYMC[2, e, :, :] * padded[e - 1]
                + BU[5] * zup(centre, 5)
                + BD[5] * zdn(centre, 5)
            )
            out.append(KEEP * centre + BC[2, e, :, :] + INVC[2, e, :, :] * total)
        return tuple(out)

    values = tuple(BC[2, e, :, :] for e in range(1, counts[2] + 1))
    values = lax.fori_loop(0, SWEEPS - 1, sweep, values)
    for e in range(1, counts[2] + 1):
        VC[2, e, :, :] = values[e - 1]
    for k in (1, 0):
        for e in range(counts[k]):
            VC[k, e + 1, :, :] = VC[k, e + 1, :, :] + VC[k + 1, e // 2 + 1, :, :]
        wrap(k, VC)
        relax_coarse(k, VC, WC)
        relax_coarse(k, WC, VC)

    for j in range(8):
        y = 4 * d + j - 2
        inside = (y >= 0) & (y < 4 * devs)
        y = jnp.minimum(jnp.maximum(y, 0), 4 * devs - 1)
        tile = VC[0, lax.rem(y, counts[0]) + 1, :, :]
        mine = jnp.where(inside, lax.div(y, counts[0]), 4)
        UU[j, :, :] = pair(pair(jnp.where(spot == mine, tile, 0.0), 1), 2)
    for x in range(8):
        for c in range(2):
            rows = [jnp.broadcast_to(UU[4 * c + k, x : x + 1, :], (8, 128)) for k in range(4)]
            fine = jnp.where(
                sub < 4, jnp.where(sub < 2, rows[0], rows[1]), jnp.where(sub < 6, rows[2], rows[3])
            )
            at = pl.ds(8 * c + 4, 8)
            for q in (2 * x + 2, 2 * x + 3):
                V2[q, at, :] = V2[q, at, :] + fine
    relax2(V2, W2, False)
    relax2(W2, V2, False)

    for i in range(8):
        for row, count in ((6, 8), (14, 4)):
            fine = V2[4 * g + i, pl.ds(row, count), :]
            for odd in range(2):
                P1[i, pl.ds(2 * (row - 6) + odd, count, stride=2), :] = fine
        for q in (2 * i + 1, 2 * i + 2):
            for c in range(3):
                rows = pl.ds(8 * c + 4, 8)
                V1[q, rows, :] = V1[q, rows, :] + P1[i, 8 * c : 8 * c + 8, :]
    for q in range(2, 16):
        relax1(V1, W1, False, q)
    for q in range(3, 15):
        relax1(W1, V1, False, q)

    for i in range(12):
        for row, count in ((6, 8), (14, 8), (22, 4)):
            coarse = V1[i + 3, pl.ds(row, 8), :]
            fine = (permute(coarse, low_z), permute(coarse, high_z))
            for h in range(2):
                for odd in range(2):
                    P0[h, i, pl.ds(2 * (row - 6) + odd, count, stride=2), :] = fine[h][0:count, :]
        for q in (2 * i, 2 * i + 1):
            if not 1 <= q <= 22:
                continue
            for h in range(2):
                for c in range(5):
                    rows = pl.ds(8 * c + 8, 8)
                    V0[h, q, rows, :] = V0[h, q, rows, :] + P0[h, i, 8 * c : 8 * c + 8, :]
    for q in range(2, 22):
        for c in range(5):
            relax0(V0, W0, False, q, c)
    for q in range(3, 21):
        for c in range(5):
            relax0(W0, V0, False, q, c)

    for x in range(16):
        for c in range(4):
            centre, left = left0(V0, x + 4, c)
            for h in range(2):
                pot_ref[x, 8 * c : 8 * c + 8, h * 128 : h * 128 + 128] = centre[h]
                res_ref[x, 8 * c : 8 * c + 8, h * 128 : h * 128 + 128] = left[h]

    for copy in first0 + late0 + first1 + late1 + first2:
        copy.wait_send()
    pltpu.make_async_copy(G.at[0 : devs - 1], G.at[0 : devs - 1], s3_send).wait()


def solution(mesh):
    groups, devs = mesh.shape["group"], mesh.shape["dev"]

    def rows(*shape):
        return pltpu.VMEM(shape + (128,), jnp.float32)

    def sems(count):
        return pltpu.SemaphoreType.DMA((count,))

    def on_device(source, plane_layer, layer_permittivity, tile_kind, kind_fill):
        vmem = pl.BlockSpec(memory_space=pltpu.VMEM)
        hbm = pl.BlockSpec(memory_space=pltpu.HBM)
        tiles = devs + 2
        coarse = rows(3, tiles, 8)
        out = jax.ShapeDtypeStruct(source.shape, jnp.float32)
        scratch = [
            pltpu.VMEM((2, 128), jnp.int32), pltpu.VMEM(tile_kind.shape, jnp.int32),
            pltpu.SMEM(layer_permittivity.shape, jnp.float32), pltpu.SMEM(kind_fill.shape, jnp.float32),
            rows(2, 24, 48), rows(2, 24, 56), rows(2, 24, 56), rows(2, 24, 56),
            rows(2, 12, 40), rows(12, 40), rows(4, 40), rows(4, 40),
            rows(4, 40), rows(4, 40), rows(4, 40), rows(4, 40), rows(6, 64),
            rows(8, 2, 32), rows(2, 12, 40),
            rows(18, 32), rows(18, 32), rows(18, 32), rows(18, 32),
            rows(18, 32), rows(18, 32), rows(6, 32), rows(6, 32),
            rows(6, 32), rows(6, 32), rows(6, 32), rows(6, 32), rows(6, 48),
            rows(4, 16), rows(8, 24),
            rows(16, 24), rows(8, 24), rows(20, 24), rows(20, 24), rows(20, 24),
            rows(16, 24), rows(16, 24), rows(8, 24), rows(8, 24),
            rows(8, 24), rows(8, 24), rows(8, 24), rows(8, 24), rows(10, 40),
            rows(8, 8),
            rows(12, 24), rows(devs, 8), rows(devs, 8), rows(devs // 2, 8), rows(devs // 4, 8),
            coarse, coarse, coarse, coarse, coarse, coarse, coarse, coarse, coarse, coarse,
            sems(4), sems(2), sems(18), sems(18), sems(18), sems(18), sems(9), sems(9), sems(9), sems(9),
            sems(3 * groups - 1), sems(3 * groups - 1),
            pltpu.SemaphoreType.DMA, pltpu.SemaphoreType.DMA,
        ]
        return pl.pallas_call(
            functools.partial(kernel, groups, devs),
            out_shape=(out, out),
            in_specs=[hbm] * 5,
            out_specs=(vmem, vmem),
            scratch_shapes=scratch,
            compiler_params=pltpu.CompilerParams(
                collective_id=0, has_side_effects=True, vmem_limit_bytes=60 * 1024 * 1024
            ),
        )(plane_layer.reshape(2, 128), tile_kind, layer_permittivity, kind_fill, source)

    in_specs = (P("group", "dev", None), P(), P(), P(), P())
    out_specs = (P("group", "dev", None), P("group", "dev", None))
    return jax.shard_map(
        on_device, mesh=mesh, in_specs=in_specs, out_specs=out_specs, check_vma=False
    )
```
